128 devices in a mesh: row: 16 (over y_lo, z, core), col: 8 (over x, y_hi).
Axes of the slice: x: 4, y: 4 (y_hi: 2, y_lo: 2; y = y_hi * 2 + y_lo), z: 4, core: 2. Of those that a mesh axis runs over, the one named last changes fastest.
Arguments:
- weather: bfloat16 [192, 1024, 1024], P(None, 'row', 'col'), may hold values from -6 to 6
- cotangent: bfloat16 [192, 1024, 1024], P(None, 'row', 'col'), may hold values from -6 to 6
- spectral_in: bfloat16 [2, 2, 96, 96], replicated, may hold values from -0.4375 to 0.4375
- spectral_bias: float32 [2, 2, 96], replicated, may hold values from -3 to 3
- spectral_out: bfloat16 [2, 2, 96, 96], replicated, may hold values from -1.75 to 1.75
- project_in: bfloat16 [192, 768], replicated, may hold values from -0.4375 to 0.4375
- project_out: bfloat16 [768, 192], replicated, may hold values from -0.21875 to 0.21875
Outputs:
- layer_out: bfloat16 [192, 1024, 1024], P(None, 'row', 'col')
- grad_weather: bfloat16 [192, 1024, 1024], P(None, 'row', 'col')
- grad_project_in: float32 [192, 768], replicated
- grad_project_out: float32 [768, 192], replicated
- grad_spectral_in: float32 [2, 2, 96, 96], replicated
- grad_spectral_out: float32 [2, 2, 96, 96], replicated
- grad_spectral_bias: float32 [2, 2, 96], replicated
The draws below stay inside these ranges and needn't reach their ends.
All inputs are finite; a program needn't handle non-finite values.
Results may differ from the reference program's by a relative error of at most 0.019.
The reference program's roundings to bfloat16 on the way count: a program that leaves them out, or rounds other values in their place, can miss the bound.
Values may be sent and summed in bfloat16 or wider, within the bound.
A program may use at most 192 MiB of HBM per device.

```python
import math
import jax
import jax.numpy as jnp
from jax import lax

H = 1024
W = 1024
NB = 2
BS = 96
C = 192
HID = 768
KH = 512
KW = 256


def level_of(stream_key, extent, split, least, top_value):
    level, own = 1.0, jax.random.fold_in(stream_key, 6)
    for axis_at, parts in split:
        draws = jnp.exp(jax.random.uniform(jax.random.fold_in(own, axis_at), (parts,), jnp.float32, least / len(split), top_value / len(split)))
        level = level * jnp.repeat(draws, extent[axis_at] // parts).reshape([-1 if axis == axis_at else 1 for axis in range(len(extent))])
    return level


def scatter_about(stream_key, dims, scale, reach, cuts=(), kind=jnp.bfloat16):
    factor_of = level_of(stream_key, dims, cuts, -0.22, 0.18) if cuts else 1.0
    values = jax.random.normal(stream_key, dims, jnp.float32) * scale * factor_of
    return jnp.minimum(jnp.maximum(values, -reach), reach).astype(kind)


def setup_inputs(seed: int = 0) -> dict:
    key_list = jax.random.split(jax.random.key(seed), 8)
    return {
        "weather": scatter_about(key_list[0], (C, H, W), 1.0, 6.0, ((1, 16), (2, 8))),
        "cotangent": scatter_about(key_list[1], (C, H, W), 1.0, 6.0, ((1, 16), (2, 8))),
        "spectral_in": scatter_about(key_list[2], (2, NB, BS, BS), (2 * BS) ** -0.5, 0.4375),
        "spectral_bias": scatter_about(key_list[3], (2, NB, BS), 0.5, 3.0, (), jnp.float32),
        "spectral_out": scatter_about(key_list[4], (2, NB, BS, BS), (BS // 8) ** -0.5, 1.75),
        "project_in": scatter_about(key_list[5], (C, HID), C ** -0.5, 0.4375),
        "project_out": scatter_about(key_list[6], (HID, C), HID ** -0.5, 0.21875),
    }


epsilon = 1e-05
threshold = 0.1

def product(form, left, right):
    return jnp.einsum(form, left.astype(jnp.float32), right.astype(jnp.float32))

def gelu_slope(values):
    return 0.5 * (1.0 + lax.erf(values * (1.0 / math.sqrt(2.0)))) + values * jnp.exp(-0.5 * values * values) * (1.0 / math.sqrt(2.0 * math.pi))

def width_tables(width, kept):
    position = jnp.arange(width, dtype=jnp.int32)
    frequency = jnp.arange(kept, dtype=jnp.int32)
    phases = position[:, None] * frequency[None, :] % width
    angles = phases.astype(jnp.float32) * (2.0 * math.pi / width)
    factor = 1.0 / math.sqrt(width)
    weight = jnp.where(frequency == 0, 1.0, 2.0).astype(jnp.float32)
    cosine = jnp.cos(angles) * factor
    sine_values = -jnp.sin(angles) * factor
    return (cosine.astype(jnp.bfloat16), sine_values.astype(jnp.bfloat16), (cosine * weight[None, :]).astype(jnp.bfloat16), (sine_values * weight[None, :]).astype(jnp.bfloat16))

def height_tables(height, kept):
    position = jnp.arange(height, dtype=jnp.int32)
    indices = jnp.arange(kept, dtype=jnp.int32)
    frequency = jnp.where(indices < kept // 2, indices, indices + (height - kept))
    phases = position[:, None] * frequency[None, :] % height
    angles = phases.astype(jnp.float32) * (2.0 * math.pi / height)
    factor = 1.0 / math.sqrt(height)
    return ((jnp.cos(angles) * factor).astype(jnp.bfloat16), (-jnp.sin(angles) * factor).astype(jnp.bfloat16))

def width_forward(field_part, cosine_table, sine_table):
    real_part = product('crw,wk->rkc', field_part, cosine_table)
    imaginary = product('crw,wk->rkc', field_part, sine_table)
    return jnp.stack([real_part, imaginary], axis=2).astype(jnp.bfloat16)

def width_inverse(spectrum, cosine_table, sine_table):
    half_width = spectrum.shape[2] // 2
    summed = product('rkc,wk->crw', spectrum[:, :, :half_width], cosine_table)
    summed = summed + product('rkc,wk->crw', spectrum[:, :, half_width:], sine_table)
    return summed.astype(jnp.bfloat16)

def height_forward(spectrum, real_table, imaginary_table):
    half_width = spectrum.shape[2] // 2
    first_term = product('hnx,hm->mnx', spectrum, real_table)
    second = product('hnx,hm->mnx', spectrum, imaginary_table)
    return jnp.concatenate([first_term[:, :, :half_width] - second[:, :, half_width:], first_term[:, :, half_width:] + second[:, :, :half_width]], axis=2)

def height_inverse(kept_modes, real_table, imaginary_table):
    half_width = kept_modes.shape[2] // 2
    first_term = product('mnx,hm->hnx', kept_modes, real_table)
    second = product('mnx,hm->hnx', kept_modes, imaginary_table)
    return jnp.concatenate([first_term[:, :, :half_width] + second[:, :, half_width:], first_term[:, :, half_width:] - second[:, :, :half_width]], axis=2)

def soft_shrink(values):
    return values - threshold * jnp.tanh(values * (1.0 / threshold))

def shrink_slope(values):
    return jnp.square(jnp.tanh(values * (1.0 / threshold)))

def spectral_forward(kept_modes, spectral_in, spectral_bias, spectral_out):
    mode_count, column_count, doubled = kept_modes.shape
    pieces = kept_modes.reshape(mode_count, column_count, 2, NB, BS)
    real_input, imaginary_input = (pieces[:, :, 0], pieces[:, :, 1])
    before_real = product('mnbi,bio->mnbo', real_input, spectral_in[0]) - product('mnbi,bio->mnbo', imaginary_input, spectral_in[1]) + spectral_bias[0]
    before_imaginary = product('mnbi,bio->mnbo', imaginary_input, spectral_in[0]) + product('mnbi,bio->mnbo', real_input, spectral_in[1]) + spectral_bias[1]
    hidden_real = jax.nn.gelu(before_real, approximate=False).astype(jnp.bfloat16)
    hidden_imaginary = jax.nn.gelu(before_imaginary, approximate=False).astype(jnp.bfloat16)
    second_real = product('mnbi,bio->mnbo', hidden_real, spectral_out[0]) - product('mnbi,bio->mnbo', hidden_imaginary, spectral_out[1])
    second_imaginary = product('mnbi,bio->mnbo', hidden_imaginary, spectral_out[0]) + product('mnbi,bio->mnbo', hidden_real, spectral_out[1])
    shrunk = jnp.stack([soft_shrink(second_real), soft_shrink(second_imaginary)], axis=2)
    shrunk = shrunk.reshape(mode_count, column_count, doubled).astype(jnp.bfloat16)
    return (shrunk, (before_real, before_imaginary, hidden_real, hidden_imaginary, second_real, second_imaginary))

def spectral_backward(gradient, kept_modes, saved, spectral_in, spectral_out):
    mode_count, column_count, doubled = gradient.shape
    grad_pieces = gradient.reshape(mode_count, column_count, 2, NB, BS)
    pieces = kept_modes.reshape(mode_count, column_count, 2, NB, BS)
    real_input, imaginary_input = (pieces[:, :, 0], pieces[:, :, 1])
    before_real, before_imaginary, hidden_real, hidden_imaginary, second_real, second_imaginary = saved
    keep_real = (grad_pieces[:, :, 0] * shrink_slope(second_real)).astype(jnp.bfloat16)
    keep_imaginary = (grad_pieces[:, :, 1] * shrink_slope(second_imaginary)).astype(jnp.bfloat16)
    back_real = product('mnbo,bio->mnbi', keep_real, spectral_out[0]) + product('mnbo,bio->mnbi', keep_imaginary, spectral_out[1])
    back_imaginary = product('mnbo,bio->mnbi', keep_imaginary, spectral_out[0]) - product('mnbo,bio->mnbi', keep_real, spectral_out[1])
    out_real = product('mnbi,mnbo->bio', hidden_real, keep_real) + product('mnbi,mnbo->bio', hidden_imaginary, keep_imaginary)
    out_imaginary = product('mnbi,mnbo->bio', hidden_real, keep_imaginary) - product('mnbi,mnbo->bio', hidden_imaginary, keep_real)
    gate_real = (back_real * gelu_slope(before_real)).astype(jnp.bfloat16)
    gate_imaginary = (back_imaginary * gelu_slope(before_imaginary)).astype(jnp.bfloat16)
    in_real = product('mnbi,mnbo->bio', real_input, gate_real) + product('mnbi,mnbo->bio', imaginary_input, gate_imaginary)
    in_imaginary = product('mnbi,mnbo->bio', real_input, gate_imaginary) - product('mnbi,mnbo->bio', imaginary_input, gate_real)
    bias_grad = jnp.stack([lax.optimization_barrier(jnp.sum(gate_real.astype(jnp.float32), axis=(0, 1))), lax.optimization_barrier(jnp.sum(gate_imaginary.astype(jnp.float32), axis=(0, 1)))])
    input_real = product('mnbo,bio->mnbi', gate_real, spectral_in[0]) + product('mnbo,bio->mnbi', gate_imaginary, spectral_in[1])
    input_imaginary = product('mnbo,bio->mnbi', gate_imaginary, spectral_in[0]) - product('mnbo,bio->mnbi', gate_real, spectral_in[1])
    grad_modes = jnp.stack([input_real, input_imaginary], axis=2)
    grad_modes = grad_modes.reshape(mode_count, column_count, doubled).astype(jnp.bfloat16)
    return (grad_modes, jnp.stack([in_real, in_imaginary]), jnp.stack([out_real, out_imaginary]), bias_grad)

def layer_norm(flat_field):
    centred = flat_field - lax.optimization_barrier(jnp.mean(flat_field, axis=0, keepdims=True))
    variance = lax.optimization_barrier(jnp.mean(centred * centred, axis=0, keepdims=True))
    inverse_spread = lax.rsqrt(variance + epsilon)
    return (centred * inverse_spread, inverse_spread)

def norm_backward(normed, inverse_spread, gradient):
    mean_grad = lax.optimization_barrier(jnp.mean(gradient, axis=0, keepdims=True))
    mean_cross = lax.optimization_barrier(jnp.mean(gradient * normed, axis=0, keepdims=True))
    return inverse_spread * (gradient - mean_grad - normed * mean_cross)

def token_block(weather, normed_in, filtered, cotangent, project_in, project_out):
    channels = weather.shape[0]
    summed = weather.astype(jnp.float32) + normed_in.astype(jnp.float32) + filtered.astype(jnp.float32)
    flat_sum = summed.reshape(channels, -1)
    normed, inverse_spread = layer_norm(flat_sum)
    normed_low = normed.astype(jnp.bfloat16)
    before = product('cn,ch->hn', normed_low, project_in)
    hidden = jax.nn.gelu(before, approximate=False).astype(jnp.bfloat16)
    output = (flat_sum + product('hn,hc->cn', hidden, project_out)).astype(jnp.bfloat16)
    flat_cot = cotangent.reshape(channels, -1)
    back_hidden = product('cn,hc->hn', flat_cot, project_out)
    back_before = (back_hidden * gelu_slope(before)).astype(jnp.bfloat16)
    grad_out = product('hn,cn->hc', hidden, flat_cot)
    grad_in = product('cn,hn->ch', normed_low, back_before)
    back_normed = product('hn,ch->cn', back_before, project_in)
    grad_sum = flat_cot.astype(jnp.float32) + norm_backward(normed, inverse_spread, back_normed)
    return (output.reshape(weather.shape), grad_sum.reshape(weather.shape), grad_in, grad_out)

def reference(weather, cotangent, spectral_in, spectral_bias, spectral_out, project_in, project_out):
    cosine, sine_table, cosine_weighted, sine_weighted = width_tables(W, KW)
    real_table, imaginary_table = height_tables(H, KH)
    block_count = 16
    block_rows = H // block_count

    def to_blocks(field_whole):
        return field_whole.reshape(C, block_count, block_rows, W).transpose(1, 0, 2, 3)

    def from_blocks(field_blocks):
        return field_blocks.transpose(1, 0, 2, 3).reshape(C, H, W)
    weather_blocks = to_blocks(weather)
    cot_blocks = to_blocks(cotangent)

    def section_one(row_block):
        normed, inverse_spread = layer_norm(row_block.astype(jnp.float32).reshape(C, -1))
        normed_low = normed.astype(jnp.bfloat16).reshape(row_block.shape)
        spectrum = width_forward(normed_low, cosine, sine_table).reshape(block_rows, KW, 2 * C)
        return (normed_low, spectrum)
    normed_blocks, spectrum = lax.map(section_one, weather_blocks)
    kept_low = height_forward(spectrum.reshape(H, KW, 2 * C), real_table, imaginary_table).astype(jnp.bfloat16)
    shrunk, saved = spectral_forward(kept_low, spectral_in, spectral_bias, spectral_out)
    back = height_inverse(shrunk, real_table, imaginary_table).astype(jnp.bfloat16)
    back = back.reshape(block_count, block_rows, KW, 2 * C)

    def section_two(pieces):
        row_block, normed_low, back_block, cot_block = pieces
        filtered = width_inverse(back_block, cosine_weighted, sine_weighted)
        output, grad_sum, grad_in, grad_out = token_block(row_block, normed_low, filtered, cot_block, project_in, project_out)
        grad_spectrum = width_forward(grad_sum.astype(jnp.bfloat16), cosine_weighted, sine_weighted)
        return (output, grad_sum, grad_spectrum.reshape(block_rows, KW, 2 * C), grad_in, grad_out)
    output, grad_sum, grad_spectrum, grad_in, grad_out = lax.map(section_two, (weather_blocks, normed_blocks, back, cot_blocks))
    grad_kept = height_forward(grad_spectrum.reshape(H, KW, 2 * C), real_table, imaginary_table)
    grad_modes, grad_first, grad_second, grad_bias = spectral_backward(grad_kept, kept_low, saved, spectral_in, spectral_out)
    grad_back = height_inverse(grad_modes, real_table, imaginary_table).astype(jnp.bfloat16)
    grad_back = grad_back.reshape(block_count, block_rows, KW, 2 * C)

    def section_three(pieces):
        row_block, grad_block, grad_back_block = pieces
        normed, inverse_spread = layer_norm(row_block.astype(jnp.float32).reshape(C, -1))
        grad_normed = grad_block + width_inverse(grad_back_block, cosine, sine_table).astype(jnp.float32)
        result = grad_block.reshape(C, -1) + norm_backward(normed, inverse_spread, grad_normed.reshape(C, -1))
        return result.reshape(row_block.shape).astype(jnp.bfloat16)
    grad_weather = lax.map(section_three, (weather_blocks, grad_sum, grad_back))
    return (from_blocks(output), from_blocks(grad_weather), lax.optimization_barrier(jnp.sum(grad_in, axis=0)) / H, lax.optimization_barrier(jnp.sum(grad_out, axis=0)) / H, grad_first / H, grad_second / H, grad_bias / H)
```

```python
from functools import partial
import math

import numpy as np
import jax
import jax.numpy as jnp
from jax import lax
from jax.experimental import pallas as pl
from jax.experimental.pallas import tpu as pltpu
from jax.sharding import PartitionSpec as P

H = 1024
W = 1024
NB = 2
BS = 96
C = 192
HID = 768
KH = 512
KW = 256

LR = 64
LW = 128
CG = 12
CH = 4
NCH = CG // CH
NX = 4
SG = 8
MODES = 2048
EPS = 1e-05
THRESHOLD = 0.1
F32 = jnp.float32
BF16 = jnp.bfloat16
MESH = pl.DeviceIdType.MESH


def tables():
    k = np.arange(KW)
    angle = (k[:, None] * np.arange(W)[None, :] % W).astype(np.float32) * np.float32(2.0 * math.pi / W)
    factor = np.float32(1.0 / math.sqrt(W))
    cosine, sine = np.cos(angle) * factor, -np.sin(angle) * factor
    width = np.stack([cosine.reshape(SG, 32, W), sine.reshape(SG, 32, W)], axis=1).reshape(2 * KW, W)
    weight = np.where(k == 0, 1.0, 2.0).astype(np.float32)[:, None]
    weighted = np.stack(
        [(cosine * weight).reshape(SG, 32, W), (sine * weight).reshape(SG, 32, W)], axis=1
    ).reshape(2 * KW, W)
    m = np.arange(KH)
    frequency = np.where(m < KH // 2, m, m + (H - KH))
    angle = (np.arange(H)[:, None] * frequency[None, :] % H).astype(np.float32) * np.float32(
        2.0 * math.pi / H
    )
    factor = np.float32(1.0 / math.sqrt(H))
    height = np.concatenate([np.cos(angle) * factor, -np.sin(angle) * factor], axis=1)
    return tuple(jnp.asarray(t, F32).astype(BF16) for t in (width, weighted, height))


def dot_nn(left, right):
    return lax.dot_general(left, right, (((1,), (0,)), ((), ())), preferred_element_type=F32)


def dot_nt(left, right):
    return lax.dot_general(left, right, (((1,), (1,)), ((), ())), preferred_element_type=F32)


def dot_tn(left, right):
    return lax.dot_general(left, right, (((0,), (0,)), ((), ())), preferred_element_type=F32)


def normal_parts(values):
    cumulative = 0.5 * (1.0 + lax.erf(values * (1.0 / math.sqrt(2.0))))
    density = jnp.exp(-0.5 * values * values) * (1.0 / math.sqrt(2.0 * math.pi))
    return cumulative, density


class Exchange:
    def __init__(self, scratch):
        (self.X, self.O, self.G, self.K, self.Y0, self.y32, self.Z0, self.Q, self.BK, self.F, self.FO) = scratch[:11]
        self.sems = scratch[11:23]
        self.ri = lax.axis_index("row")
        self.ci = lax.axis_index("col")
        self.core = self.ri % 2
        self.s = self.ri // 2
        self.x = self.ci // 2
        self.yh = self.ci % 2
        self.id1 = self.ci * 2 + self.core
        self.id2 = self.x * 2 + self.core

    def peer1(self, d):
        other = (self.id1 + d) % 16
        return other // 2, other % 2

    def peer2(self, e):
        other = (self.id2 + e) % 8
        return other // 2, other % 2

    def barrier(self):
        sem = pltpu.get_barrier_semaphore()
        for d in range(1, 16):
            col, core = self.peer1(d)
            pl.semaphore_signal(sem, inc=1, device_id=(2 * self.s + core, col), device_id_type=MESH)
        for e in range(1, SG):
            s = (self.s + e) % SG
            pl.semaphore_signal(sem, inc=1, device_id=(2 * s + self.core, self.ci), device_id_type=MESH)
        pl.semaphore_wait(sem, 15 + SG - 1)

    def first_channel(self, col, core):
        return (col % 2) * BS + (col // 2) * (2 * CG) + core * CG

    def copy1(self, src, i, d):
        col, core = self.peer1(d)
        start = self.first_channel(col, core) + i * CH
        rows = pl.ds(pl.multiple_of(self.core * LR, LR), LR)
        return pltpu.make_async_remote_copy(
            src_ref=src.at[pl.ds(start, CH)],
            dst_ref=self.X.at[self.ci, pl.ds(i * CH, CH), rows, :],
            send_sem=self.sems[0].at[i, d],
            recv_sem=self.sems[1].at[i, d],
            device_id=(2 * self.s + core, col),
            device_id_type=MESH,
        )

    def send1(self, src):
        rows = pl.ds(pl.multiple_of(self.core * LR, LR), LR)
        own = self.first_channel(self.ci, self.core)
        for i in range(NCH):
            for d in range(1, 16):
                self.copy1(src, i, d).start()
        self.X[self.ci, :, rows, :] = src[pl.ds(own, CG)]

    def copyb(self, i, e):
        s = (self.s + e) % SG
        return pltpu.make_async_remote_copy(
            src_ref=self.O.at[s, pl.ds(i * CH, CH)],
            dst_ref=self.G.at[self.s, pl.ds(i * CH, CH)],
            send_sem=self.sems[2].at[i, e],
            recv_sem=self.sems[3].at[i, e],
            device_id=(2 * s + self.core, self.ci),
            device_id_type=MESH,
        )

    def width_forward(self, src, table):
        @pl.loop(0, NCH)
        def _(i):
            for d in range(1, 16):
                self.copy1(src, i, d).wait_recv()
            for half in range(CH // 2):
                c = i * CH + 2 * half
                field = jnp.concatenate(
                    [self.X[p, pl.ds(c, 2)].reshape(2 * 2 * LR, LW) for p in range(8)], axis=1
                )
                spectrum = dot_nt(table[...], field).astype(BF16)
                for j in range(2):
                    self.O[:, c + j] = spectrum[:, j * 128 : (j + 1) * 128].reshape(SG, 64, 128)
            for e in range(1, SG):
                self.copyb(i, e).start()
            own = pl.ds(i * CH, CH)
            self.G[self.s, own] = self.O[self.s, own]

    def copyc(self, i, e):
        x, core = self.peer2(e)
        return pltpu.make_async_remote_copy(
            src_ref=self.K.at[x, core, pl.ds(i * CH, CH)],
            dst_ref=self.Y0.at[self.id2, pl.ds(i * CH, CH)],
            send_sem=self.sems[4].at[i, e],
            recv_sem=self.sems[5].at[i, e],
            device_id=(2 * self.s + core, 2 * x + self.yh),
            device_id_type=MESH,
        )

    def height_forward(self, table):
        @pl.loop(0, NCH)
        def _(i):
            for e in range(1, SG):
                self.copyb(i, e).wait_recv()
            own = pl.ds(i * CH, CH)
            spectrum = jnp.concatenate(
                [self.G[s, own].reshape(CH * 64, 128) for s in range(SG)], axis=1
            )
            for x in range(NX):
                lanes = slice(x * 128, (x + 1) * 128)
                shifted = slice(KH + x * 128, KH + (x + 1) * 128)
                both = jnp.concatenate([table[:, lanes], table[:, shifted]], axis=1)
                terms = dot_nn(spectrum, both).reshape(CH, 2, 2, 16, 256)
                real = terms[:, 0, :, :, :128] - terms[:, 1, :, :, 128:]
                imaginary = terms[:, 0, :, :, 128:] + terms[:, 1, :, :, :128]
                for core in range(2):
                    self.K[x, core, own, 0] = real[:, core].astype(BF16)
                    self.K[x, core, own, 1] = imaginary[:, core].astype(BF16)
            for e in range(1, 8):
                self.copyc(i, e).start()
            self.Y0[self.id2, own] = self.K[self.x, self.core, own]

    def modes(self, out):
        @pl.loop(0, NCH)
        def _(i):
            for e in range(1, 8):
                self.copyc(i, e).wait_recv()
        self.y32[...] = self.Y0[...].astype(F32).reshape(BS * 32, 128)
        for part in range(2):
            for k in range(16):
                out[part * BS : (part + 1) * BS, k * 128 : (k + 1) * 128] = self.y32[
                    pl.ds(part * 16 + k, BS, stride=32), :
                ].astype(BF16)

    def copyz(self, e):
        x, core = self.peer2(e)
        return pltpu.make_async_remote_copy(
            src_ref=self.Z0.at[x * 2 + core],
            dst_ref=self.Q.at[self.x, :, :, pl.ds(pl.multiple_of(self.core * 16, 16), 16), :],
            send_sem=self.sems[6].at[e],
            recv_sem=self.sems[7].at[e],
            device_id=(2 * self.s + core, 2 * x + self.yh),
            device_id_type=MESH,
        )

    def from_modes(self, values):
        for q in range(4):
            block = values(q * 512, (q + 1) * 512)
            for part in range(2):
                for j in range(4):
                    self.y32[pl.ds(part * 16 + q * 4 + j, BS, stride=32), :] = block[
                        part * BS : (part + 1) * BS, j * 128 : (j + 1) * 128
                    ]
        self.Z0[...] = self.y32[...].astype(BF16).reshape(8, CG, 2, 16, 128)
        for e in range(1, 8):
            self.copyz(e).start()
        self.Q[self.x, :, :, pl.ds(pl.multiple_of(self.core * 16, 16), 16), :] = self.Z0[self.id2]

    def copyf(self, i, e):
        s = (self.s + e) % SG
        return pltpu.make_async_remote_copy(
            src_ref=self.BK.at[s, pl.ds(i * CH, CH)],
            dst_ref=self.F.at[self.s, pl.ds(i * CH, CH)],
            send_sem=self.sems[8].at[i, e],
            recv_sem=self.sems[9].at[i, e],
            device_id=(2 * s + self.core, self.ci),
            device_id_type=MESH,
        )

    def height_inverse(self, table):
        for e in range(1, 8):
            self.copyz(e).wait_recv()

        @pl.loop(0, NCH)
        def _(i):
            own = pl.ds(i * CH, CH)
            modes = jnp.concatenate([self.Q[x, own].reshape(CH * 64, 128) for x in range(NX)], axis=1)
            for q in range(4):
                rows = slice(q * 256, (q + 1) * 256)
                first = dot_nt(modes, table[rows, :KH]).reshape(CH, 2, 32, 256)
                second = dot_nt(modes, table[rows, KH:]).reshape(CH, 2, 32, 256)
                real = (first[:, 0] + second[:, 1]).astype(BF16)
                imaginary = (first[:, 1] - second[:, 0]).astype(BF16)
                for j in range(2):
                    lanes = slice(j * 128, (j + 1) * 128)
                    self.BK[2 * q + j, own, :32, :] = real[:, :, lanes]
                    self.BK[2 * q + j, own, 32:, :] = imaginary[:, :, lanes]
            for e in range(1, SG):
                self.copyf(i, e).start()
            self.F[self.s, own] = self.BK[self.s, own]

    def copyo(self, out, i, d):
        col, core = self.peer1(d)
        start = self.first_channel(self.ci, self.core) + i * CH
        rows = pl.ds(pl.multiple_of(core * LR, LR), LR)
        return pltpu.make_async_remote_copy(
            src_ref=self.FO.at[col, pl.ds(i * CH, CH), rows, :],
            dst_ref=out.at[pl.ds(start, CH)],
            send_sem=self.sems[10].at[i, d],
            recv_sem=self.sems[11].at[i, d],
            device_id=(2 * self.s + core, col),
            device_id_type=MESH,
        )

    def width_inverse(self, out, table):
        rows = pl.ds(pl.multiple_of(self.core * LR, LR), LR)
        start = self.first_channel(self.ci, self.core)

        @pl.loop(0, NCH)
        def _(i):
            for e in range(1, SG):
                self.copyf(i, e).wait_recv()
            for half in range(CH // 2):
                c = i * CH + 2 * half
                spectrum = jnp.concatenate(
                    [self.F[:, c].reshape(2 * KW, 128), self.F[:, c + 1].reshape(2 * KW, 128)], axis=1
                )
                turned = spectrum.T
                for q in range(4):
                    field = dot_nn(turned, table[:, q * 256 : (q + 1) * 256]).astype(BF16)
                    for j in range(2):
                        self.FO[2 * q + j, pl.ds(c, 2)] = field[:, j * 128 : (j + 1) * 128].reshape(
                            2, 128, 128
                        )
            for d in range(1, 16):
                self.copyo(out, i, d).start()
            out[pl.ds(start + i * CH, CH)] = self.FO[self.ci, pl.ds(i * CH, CH), rows, :]

    def finish(self, src, out):
        @pl.loop(0, NCH)
        def _(i):
            for d in range(1, 16):
                self.copyo(out, i, d).wait_recv()
        self.drain(src, out)

    def drain(self, src, out):
        @pl.loop(0, NCH)
        def _(i):
            for d in range(1, 16):
                self.copy1(src, i, d).wait_send()
                self.copyo(out, i, d).wait_send()
            for e in range(1, 8):
                self.copyb(i, e).wait_send()
                self.copyc(i, e).wait_send()
                self.copyf(i, e).wait_send()
        for e in range(1, 8):
            self.copyz(e).wait_send()


def exchange_scratch():
    dma = pltpu.SemaphoreType.DMA
    pairs = [(NCH, 16), (NCH, 8), (NCH, 8), (8,), (NCH, 8), (NCH, 16)]
    return [
        pltpu.VMEM((8, CG, 2 * LR, LW), BF16),
        pltpu.VMEM((SG, CG, 64, 128), BF16),
        pltpu.VMEM((SG, CG, 64, 128), BF16),
        pltpu.VMEM((NX, 2, CG, 2, 16, 128), BF16),
        pltpu.VMEM((8, CG, 2, 16, 128), BF16),
        pltpu.VMEM((BS * 32, 128), F32),
        pltpu.VMEM((8, CG, 2, 16, 128), BF16),
        pltpu.VMEM((NX, CG, 2, 32, 128), BF16),
        pltpu.VMEM((SG, CG, 64, 128), BF16),
        pltpu.VMEM((SG, CG, 64, 128), BF16),
        pltpu.VMEM((8, CG, 2 * LR, LW), BF16),
    ] + [dma(shape) for shape in pairs for _ in range(2)]


def channel_mean(read):
    total = read(0)
    for c in range(1, C):
        total = total + read(c)
    return total * (1.0 / C)


def norm_rows(field, rows):
    mean = channel_mean(lambda c: field[c, rows, :].astype(F32))

    def square(c):
        centred = field[c, rows, :].astype(F32) - mean
        return centred * centred

    return mean, lax.rsqrt(channel_mean(square) + EPS)


def forward_kernel(
    weather, width, weighted, height, mix_in, bias, mix_out,
    normed, filtered, kept, before_out, hidden_out, slope_out, *scratch
):
    ex = Exchange(scratch)

    @pl.loop(0, LR // 16)
    def _(r):
        rows = pl.ds(pl.multiple_of(r * 16, 16), 16)
        mean, spread = norm_rows(weather, rows)
        for c in range(C):
            normed[c, rows, :] = ((weather[c, rows, :].astype(F32) - mean) * spread).astype(BF16)

    ex.barrier()
    ex.send1(normed)
    ex.width_forward(normed, width)
    ex.height_forward(height)
    ex.modes(kept)

    def mixed(lo, hi):
        before = dot_nn(mix_in[...], kept[:, lo:hi]) + bias[...]
        before_out[:, lo:hi] = before
        cumulative, _ = normal_parts(before)
        hidden = (before * cumulative).astype(BF16)
        hidden_out[:, lo:hi] = hidden
        second = dot_nn(mix_out[...], hidden)
        slope = jnp.tanh(second * (1.0 / THRESHOLD))
        slope_out[:, lo:hi] = slope
        return second - THRESHOLD * slope

    ex.from_modes(mixed)
    ex.height_inverse(height)
    ex.width_inverse(filtered, weighted)
    ex.finish(normed, filtered)


def backward_kernel(
    weather, grad_sum, width, weighted, height, mix_in_t, mix_out_t, kept, before, hidden, slope,
    grad_weather, grad_in, grad_out, grad_bias, low, filtered, grads, gate, *scratch
):
    ex = Exchange(scratch)

    @pl.loop(0, LR // 16)
    def _(r):
        rows = pl.ds(pl.multiple_of(r * 16, 16), 16)
        for c in range(C):
            low[c, rows, :] = grad_sum[c, rows, :].astype(BF16)

    ex.barrier()
    ex.send1(low)
    ex.width_forward(low, weighted)
    ex.height_forward(height)
    ex.modes(grads)

    def mixed(lo, hi):
        factor = slope[:, lo:hi]
        second = (grads[:, lo:hi].astype(F32) * (factor * factor)).astype(BF16)
        grads[:, lo:hi] = second
        back = dot_nn(mix_out_t[...], second)
        values = before[:, lo:hi]
        cumulative, density = normal_parts(values)
        gated = (back * (cumulative + values * density)).astype(BF16)
        gate[:, lo:hi] = gated
        return dot_nn(mix_in_t[...], gated)

    ex.from_modes(mixed)
    grad_out[...] = dot_nt(hidden[...], grads[...])
    grad_in[...] = dot_nt(kept[...], gate[...])
    grad_bias[...] = jnp.sum(gate[...].astype(F32), axis=1, keepdims=True)
    ex.height_inverse(height)
    ex.width_inverse(filtered, width)
    ex.finish(low, filtered)

    @pl.loop(0, LR // 16)
    def _(r):
        rows = pl.ds(pl.multiple_of(r * 16, 16), 16)
        mean, spread = norm_rows(weather, rows)

        def total(c):
            return grad_sum[c, rows, :] + filtered[c, rows, :].astype(F32)

        def normal(c):
            return (weather[c, rows, :].astype(F32) - mean) * spread

        mean_grad = channel_mean(total)
        mean_cross = channel_mean(lambda c: total(c) * normal(c))
        for c in range(C):
            inner = total(c) - mean_grad - normal(c) * mean_cross
            grad_weather[c, rows, :] = (grad_sum[c, rows, :] + spread * inner).astype(BF16)


TR = 16
TN = TR * LW
CHUNK = 512


def token_kernel(
    weather, normed_in, filtered, cotangent, pin, pin_t, pout, pout_t,
    output, grad_sum, acc_in, acc_out, s32, x32, c32, g32, normal_low, cot_low
):
    step = pl.program_id(0)

    @pl.when(step == 0)
    def _():
        acc_in[...] = jnp.zeros_like(acc_in)
        acc_out[...] = jnp.zeros_like(acc_out)

    def at(c):
        return slice(c * TR, (c + 1) * TR)

    total = jnp.zeros((TR, LW), F32)
    for c in range(C):
        value = weather[c].astype(F32) + normed_in[c].astype(F32) + filtered[c].astype(F32)
        s32[at(c), :] = value
        total = total + value
        c32[at(c), :] = cotangent[c].astype(F32)
    mean = total * (1.0 / C)

    def square(c):
        centred = s32[at(c), :] - mean
        return centred * centred

    spread = lax.rsqrt(channel_mean(square) + EPS)
    for c in range(C):
        x32[at(c), :] = (s32[at(c), :] - mean) * spread
    for j in range(TR):
        lanes = slice(j * LW, (j + 1) * LW)
        normal_low[:, lanes] = x32[pl.ds(j, C, stride=TR), :].astype(BF16)
        cot_low[:, lanes] = c32[pl.ds(j, C, stride=TR), :].astype(BF16)

    @pl.loop(0, TN // CHUNK)
    def _(q):
        lanes = pl.ds(pl.multiple_of(q * CHUNK, CHUNK), CHUNK)
        normal = normal_low[:, lanes]
        cot = cot_low[:, lanes]
        before = dot_nn(pin_t[...], normal)
        cumulative, density = normal_parts(before)
        hidden = (before * cumulative).astype(BF16)
        back_hidden = dot_nn(pout[...], cot)
        back_before = (back_hidden * (cumulative + before * density)).astype(BF16)
        out = dot_nn(pout_t[...], hidden)
        back_normed = dot_nn(pin[...], back_before)
        acc_out[...] += dot_nt(hidden, cot)
        acc_in[...] += dot_nt(back_before, normal)
        for j in range(CHUNK // LW):
            sl = slice(j * LW, (j + 1) * LW)
            where = pl.ds(q * (CHUNK // LW) + j, C, stride=TR)
            s32[where, :] += out[:, sl]
            g32[where, :] = back_normed[:, sl]

    for c in range(C):
        output[c] = s32[at(c), :].astype(BF16)
    mean_grad = channel_mean(lambda c: g32[at(c), :])
    mean_cross = channel_mean(lambda c: g32[at(c), :] * x32[at(c), :])
    for c in range(C):
        inner = g32[at(c), :] - mean_grad - x32[at(c), :] * mean_cross
        grad_sum[c] = c32[at(c), :] + spread * inner


def vmem():
    return pl.BlockSpec(memory_space=pltpu.VMEM)


def forward_call(weather, width, weighted, height, mix_in, bias, mix_out):
    shape = jax.ShapeDtypeStruct
    return pl.pallas_call(
        forward_kernel,
        out_shape=(
            shape((C, LR, LW), BF16),
            shape((C, LR, LW), BF16),
            shape((C, MODES), BF16),
            shape((C, MODES), F32),
            shape((C, MODES), BF16),
            shape((C, MODES), F32),
        ),
        in_specs=[vmem()] * 7,
        out_specs=[vmem()] * 6,
        scratch_shapes=exchange_scratch(),
        compiler_params=pltpu.CompilerParams(
            collective_id=0, has_side_effects=True, vmem_limit_bytes=60 << 20
        ),
        name="spectral_forward",
    )(weather, width, weighted, height, mix_in, bias, mix_out)


def backward_call(*args):
    shape = jax.ShapeDtypeStruct
    return pl.pallas_call(
        backward_kernel,
        out_shape=(
            shape((C, LR, LW), BF16),
            shape((C, C), F32),
            shape((C, C), F32),
            shape((C, 1), F32),
        ),
        in_specs=[vmem()] * 11,
        out_specs=[vmem()] * 4,
        scratch_shapes=[
            pltpu.VMEM((C, LR, LW), BF16),
            pltpu.VMEM((C, LR, LW), BF16),
            pltpu.VMEM((C, MODES), BF16),
            pltpu.VMEM((C, MODES), BF16),
        ]
        + exchange_scratch(),
        compiler_params=pltpu.CompilerParams(
            collective_id=1, has_side_effects=True, vmem_limit_bytes=63 << 20
        ),
        name="spectral_backward",
    )(*args)


def token_call(weather, normed_in, filtered, cotangent, pin, pin_t, pout, pout_t):
    shape = jax.ShapeDtypeStruct
    block = pl.BlockSpec((C, TR, LW), lambda i: (0, i, 0))

    def whole(*dims):
        return pl.BlockSpec(dims, lambda i: (0,) * len(dims))

    return pl.pallas_call(
        token_kernel,
        grid=(LR // TR,),
        out_shape=(
            shape((C, LR, LW), BF16),
            shape((C, LR, LW), F32),
            shape((HID, C), F32),
            shape((HID, C), F32),
        ),
        in_specs=[block] * 4 + [whole(C, HID), whole(HID, C), whole(HID, C), whole(C, HID)],
        out_specs=[block, block, whole(HID, C), whole(HID, C)],
        scratch_shapes=[pltpu.VMEM((C * TR, LW), F32)] * 4 + [pltpu.VMEM((C, TN), BF16)] * 2,
        compiler_params=pltpu.CompilerParams(vmem_limit_bytes=60 << 20),
        name="token_block",
    )(weather, normed_in, filtered, cotangent, pin, pin_t, pout, pout_t)


def mixing(weights):
    real, imaginary = weights[0].T, weights[1].T
    return jnp.concatenate(
        [
            jnp.concatenate([real, -imaginary], axis=1),
            jnp.concatenate([imaginary, real], axis=1),
        ],
        axis=0,
    )


def complex_grad(pairs):
    return jnp.stack(
        [
            pairs[:BS, :BS] + pairs[BS:, BS:],
            pairs[:BS, BS:] - pairs[BS:, :BS],
        ]
    )


def body(weather, cotangent, spectral_in, spectral_bias, spectral_out, project_in, project_out):
    width, weighted, height = tables()
    block = lax.axis_index("col") % 2
    mix_in = mixing(lax.dynamic_index_in_dim(spectral_in, block, axis=1, keepdims=False))
    mix_out = mixing(lax.dynamic_index_in_dim(spectral_out, block, axis=1, keepdims=False))
    bias = lax.dynamic_index_in_dim(spectral_bias, block, axis=1, keepdims=False).reshape(C, 1)
    normed, filtered, kept, before, hidden, slope = forward_call(
        weather, width, weighted, height, mix_in, bias, mix_out
    )
    output, grad_sum, acc_in, acc_out = token_call(
        weather, normed, filtered, cotangent, project_in, project_in.T, project_out, project_out.T
    )
    early = lax.psum(jnp.stack([acc_in, acc_out]), ("row", "col"))
    grad_weather, grad_first, grad_second, grad_bias = backward_call(
        weather, grad_sum, width, weighted, height, mix_in.T, mix_out.T, kept, before, hidden, slope
    )
    late = jnp.concatenate(
        [
            complex_grad(grad_first).reshape(-1),
            complex_grad(grad_second).reshape(-1),
            grad_bias.reshape(-1),
        ]
    )
    slots = jnp.where(jnp.arange(2)[:, None] == block, late[None, :], 0.0)
    late = lax.psum(slots, ("row", "col"))
    size = 2 * BS * BS
    grad_spectral_in = late[:, :size].reshape(2, 2, BS, BS).transpose(1, 0, 2, 3)
    grad_spectral_out = late[:, size : 2 * size].reshape(2, 2, BS, BS).transpose(1, 0, 2, 3)
    grad_spectral_bias = late[:, 2 * size :].reshape(2, 2, BS).transpose(1, 0, 2)
    return (
        output,
        grad_weather,
        early[0].T / H,
        early[1] / H,
        grad_spectral_in / H,
        grad_spectral_out / H,
        grad_spectral_bias / H,
    )


def solution(mesh):
    in_specs = (P(None, "row", "col"), P(None, "row", "col"), P(), P(), P(), P(), P())
    out_specs = (P(None, "row", "col"), P(None, "row", "col"), P(), P(), P(), P(), P())
    return jax.shard_map(body, mesh=mesh, in_specs=in_specs, out_specs=out_specs, check_vma=False)
```

```python
from functools import partial
import math

import numpy as np
import jax
import jax.numpy as jnp
from jax import lax
from jax.experimental import pallas as pl
from jax.experimental.pallas import tpu as pltpu
from jax.sharding import PartitionSpec as P

H = 1024
W = 1024
NB = 2
BS = 96
C = 192
HID = 768
KH = 512
KW = 256

LR = 64
LW = 128
CG = 12
CH = 4
NCH = CG // CH
NX = 4
SG = 8
MODES = 2048
EPS = 1e-05
THRESHOLD = 0.1
F32 = jnp.float32
BF16 = jnp.bfloat16
MESH = pl.DeviceIdType.MESH


def tables():
    k = np.arange(KW)
    angle = (k[:, None] * np.arange(W)[None, :] % W).astype(np.float32) * np.float32(2.0 * math.pi / W)
    factor = np.float32(1.0 / math.sqrt(W))
    cosine, sine = np.cos(angle) * factor, -np.sin(angle) * factor
    width = np.stack([cosine.reshape(SG, 32, W), sine.reshape(SG, 32, W)], axis=1).reshape(2 * KW, W)
    weight = np.where(k == 0, 1.0, 2.0).astype(np.float32)[:, None]
    weighted = np.stack(
        [(cosine * weight).reshape(SG, 32, W), (sine * weight).reshape(SG, 32, W)], axis=1
    ).reshape(2 * KW, W)
    m = np.arange(KH)
    frequency = np.where(m < KH // 2, m, m + (H - KH))
    angle = (np.arange(H)[:, None] * frequency[None, :] % H).astype(np.float32) * np.float32(
        2.0 * math.pi / H
    )
    factor = np.float32(1.0 / math.sqrt(H))
    height = np.concatenate([np.cos(angle) * factor, -np.sin(angle) * factor], axis=1)
    return tuple(jnp.asarray(t, F32).astype(BF16) for t in (width, weighted, height))


def dot_nn(left, right):
    return lax.dot_general(left, right, (((1,), (0,)), ((), ())), preferred_element_type=F32)


def dot_nt(left, right):
    return lax.dot_general(left, right, (((1,), (1,)), ((), ())), preferred_element_type=F32)


def dot_tn(left, right):
    return lax.dot_general(left, right, (((0,), (0,)), ((), ())), preferred_element_type=F32)


def normal_parts(values):
    cumulative = 0.5 * (1.0 + lax.erf(values * (1.0 / math.sqrt(2.0))))
    density = jnp.exp(-0.5 * values * values) * (1.0 / math.sqrt(2.0 * math.pi))
    return cumulative, density


class Exchange:
    def __init__(self, scratch):
        (self.X, self.O, self.G, self.K, self.Y0, self.y32, self.Z0, self.Q, self.BK, self.F, self.FO) = scratch[:11]
        self.sems = scratch[11:23]
        self.ri = lax.axis_index("row")
        self.ci = lax.axis_index("col")
        self.core = self.ri % 2
        self.s = self.ri // 2
        self.x = self.ci // 2
        self.yh = self.ci % 2
        self.id1 = self.ci * 2 + self.core
        self.id2 = self.x * 2 + self.core

    def peer1(self, d):
        other = (self.id1 + d) % 16
        return other // 2, other % 2

    def peer2(self, e):
        other = (self.id2 + e) % 8
        return other // 2, other % 2

    def barrier(self):
        sem = pltpu.get_barrier_semaphore()
        for d in range(1, 16):
            col, core = self.peer1(d)
            pl.semaphore_signal(sem, inc=1, device_id=(2 * self.s + core, col), device_id_type=MESH)
        for e in range(1, SG):
            s = (self.s + e) % SG
            pl.semaphore_signal(sem, inc=1, device_id=(2 * s + self.core, self.ci), device_id_type=MESH)
        pl.semaphore_wait(sem, 15 + SG - 1)

    def first_channel(self, col, core):
        return (col % 2) * BS + (col // 2) * (2 * CG) + core * CG

    def copy1(self, src, i, d):
        col, core = self.peer1(d)
        start = self.first_channel(col, core) + i * CH
        rows = pl.ds(pl.multiple_of(self.core * LR, LR), LR)
        return pltpu.make_async_remote_copy(
            src_ref=src.at[pl.ds(start, CH)],
            dst_ref=self.X.at[self.ci, pl.ds(i * CH, CH), rows, :],
            send_sem=self.sems[0].at[i, d],
            recv_sem=self.sems[1].at[i, d],
            device_id=(2 * self.s + core, col),
            device_id_type=MESH,
        )

    def send1(self, src):
        rows = pl.ds(pl.multiple_of(self.core * LR, LR), LR)
        own = self.first_channel(self.ci, self.core)
        for i in range(NCH):
            for d in range(1, 16):
                self.copy1(src, i, d).start()
        self.X[self.ci, :, rows, :] = src[pl.ds(own, CG)]

    def copyb(self, i, e):
        s = (self.s + e) % SG
        return pltpu.make_async_remote_copy(
            src_ref=self.O.at[s, pl.ds(i * CH, CH)],
            dst_ref=self.G.at[self.s, pl.ds(i * CH, CH)],
            send_sem=self.sems[2].at[i, e],
            recv_sem=self.sems[3].at[i, e],
            device_id=(2 * s + self.core, self.ci),
            device_id_type=MESH,
        )

    def width_forward(self, src, table):
        @pl.loop(0, NCH)
        def _(i):
            for d in range(1, 16):
                self.copy1(src, i, d).wait_recv()
            for half in range(CH // 2):
                c = i * CH + 2 * half
                field = jnp.concatenate(
                    [self.X[p, pl.ds(c, 2)].reshape(2 * 2 * LR, LW) for p in range(8)], axis=1
                )
                spectrum = dot_nt(table[...], field).astype(BF16)
                for j in range(2):
                    self.O[:, c + j] = spectrum[:, j * 128 : (j + 1) * 128].reshape(SG, 64, 128)
            for e in range(1, SG):
                self.copyb(i, e).start()
            own = pl.ds(i * CH, CH)
            self.G[self.s, own] = self.O[self.s, own]

    def copyc(self, i, e):
        x, core = self.peer2(e)
        return pltpu.make_async_remote_copy(
            src_ref=self.K.at[x, core, pl.ds(i * CH, CH)],
            dst_ref=self.Y0.at[self.id2, pl.ds(i * CH, CH)],
            send_sem=self.sems[4].at[i, e],
            recv_sem=self.sems[5].at[i, e],
            device_id=(2 * self.s + core, 2 * x + self.yh),
            device_id_type=MESH,
        )

    def height_forward(self, table):
        @pl.loop(0, NCH)
        def _(i):
            for e in range(1, SG):
                self.copyb(i, e).wait_recv()
            own = pl.ds(i * CH, CH)
            spectrum = jnp.concatenate(
                [self.G[s, own].reshape(CH * 64, 128) for s in range(SG)], axis=1
            )
            for x in range(NX):
                lanes = slice(x * 128, (x + 1) * 128)
                shifted = slice(KH + x * 128, KH + (x + 1) * 128)
                both = jnp.concatenate([table[:, lanes], table[:, shifted]], axis=1)
                terms = dot_nn(spectrum, both).reshape(CH, 2, 2, 16, 256)
                real = terms[:, 0, :, :, :128] - terms[:, 1, :, :, 128:]
                imaginary = terms[:, 0, :, :, 128:] + terms[:, 1, :, :, :128]
                for core in range(2):
                    self.K[x, core, own, 0] = real[:, core].astype(BF16)
                    self.K[x, core, own, 1] = imaginary[:, core].astype(BF16)
            for e in range(1, 8):
                self.copyc(i, e).start()
            self.Y0[self.id2, own] = self.K[self.x, self.core, own]

    def modes(self, out):
        @pl.loop(0, NCH)
        def _(i):
            for e in range(1, 8):
                self.copyc(i, e).wait_recv()
        self.y32[...] = self.Y0[...].astype(F32).reshape(BS * 32, 128)
        for part in range(2):
            for k in range(16):
                out[part * BS : (part + 1) * BS, k * 128 : (k + 1) * 128] = self.y32[
                    pl.ds(part * 16 + k, BS, stride=32), :
                ].astype(BF16)

    def copyz(self, e):
        x, core = self.peer2(e)
        return pltpu.make_async_remote_copy(
            src_ref=self.Z0.at[x * 2 + core],
            dst_ref=self.Q.at[self.x, :, :, pl.ds(pl.multiple_of(self.core * 16, 16), 16), :],
            send_sem=self.sems[6].at[e],
            recv_sem=self.sems[7].at[e],
            device_id=(2 * self.s + core, 2 * x + self.yh),
            device_id_type=MESH,
        )

    def from_modes(self, values):
        for q in range(4):
            block = values(q * 512, (q + 1) * 512)
            for part in range(2):
                for j in range(4):
                    self.y32[pl.ds(part * 16 + q * 4 + j, BS, stride=32), :] = block[
                        part * BS : (part + 1) * BS, j * 128 : (j + 1) * 128
                    ]
        self.Z0[...] = self.y32[...].astype(BF16).reshape(8, CG, 2, 16, 128)
        for e in range(1, 8):
            self.copyz(e).start()
        self.Q[self.x, :, :, pl.ds(pl.multiple_of(self.core * 16, 16), 16), :] = self.Z0[self.id2]

    def copyf(self, i, e):
        s = (self.s + e) % SG
        return pltpu.make_async_remote_copy(
            src_ref=self.BK.at[s, pl.ds(i * CH, CH)],
            dst_ref=self.F.at[self.s, pl.ds(i * CH, CH)],
            send_sem=self.sems[8].at[i, e],
            recv_sem=self.sems[9].at[i, e],
            device_id=(2 * s + self.core, self.ci),
            device_id_type=MESH,
        )

    def height_inverse(self, table):
        for e in range(1, 8):
            self.copyz(e).wait_recv()

        @pl.loop(0, NCH)
        def _(i):
            own = pl.ds(i * CH, CH)
            modes = jnp.concatenate([self.Q[x, own].reshape(CH * 64, 128) for x in range(NX)], axis=1)
            for q in range(4):
                rows = slice(q * 256, (q + 1) * 256)
                first = dot_nt(modes, table[rows, :KH]).reshape(CH, 2, 32, 256)
                second = dot_nt(modes, table[rows, KH:]).reshape(CH, 2, 32, 256)
                real = (first[:, 0] + second[:, 1]).astype(BF16)
                imaginary = (first[:, 1] - second[:, 0]).astype(BF16)
                for j in range(2):
                    lanes = slice(j * 128, (j + 1) * 128)
                    self.BK[2 * q + j, own, :32, :] = real[:, :, lanes]
                    self.BK[2 * q + j, own, 32:, :] = imaginary[:, :, lanes]
            for e in range(1, SG):
                self.copyf(i, e).start()
            self.F[self.s, own] = self.BK[self.s, own]

    def copyo(self, out, i, d):
        col, core = self.peer1(d)
        start = self.first_channel(self.ci, self.core) + i * CH
        rows = pl.ds(pl.multiple_of(core * LR, LR), LR)
        return pltpu.make_async_remote_copy(
            src_ref=self.FO.at[col, pl.ds(i * CH, CH), rows, :],
            dst_ref=out.at[pl.ds(start, CH)],
            send_sem=self.sems[10].at[i, d],
            recv_sem=self.sems[11].at[i, d],
            device_id=(2 * self.s + core, col),
            device_id_type=MESH,
        )

    def width_inverse(self, out, table):
        rows = pl.ds(pl.multiple_of(self.core * LR, LR), LR)
        start = self.first_channel(self.ci, self.core)

        @pl.loop(0, NCH)
        def _(i):
            for e in range(1, SG):
                self.copyf(i, e).wait_recv()
            for half in range(CH // 2):
                c = i * CH + 2 * half
                spectrum = jnp.concatenate(
                    [self.F[:, c].reshape(2 * KW, 128), self.F[:, c + 1].reshape(2 * KW, 128)], axis=1
                )
                turned = spectrum.T
                for q in range(4):
                    field = dot_nn(turned, table[:, q * 256 : (q + 1) * 256]).astype(BF16)
                    for j in range(2):
                        self.FO[2 * q + j, pl.ds(c, 2)] = field[:, j * 128 : (j + 1) * 128].reshape(
                            2, 128, 128
                        )
            for d in range(1, 16):
                self.copyo(out, i, d).start()
            out[pl.ds(start + i * CH, CH)] = self.FO[self.ci, pl.ds(i * CH, CH), rows, :]

    def finish(self, src, out):
        @pl.loop(0, NCH)
        def _(i):
            for d in range(1, 16):
                self.copyo(out, i, d).wait_recv()
        self.drain(src, out)

    def drain(self, src, out):
        @pl.loop(0, NCH)
        def _(i):
            for d in range(1, 16):
                self.copy1(src, i, d).wait_send()
                self.copyo(out, i, d).wait_send()
            for e in range(1, 8):
                self.copyb(i, e).wait_send()
                self.copyc(i, e).wait_send()
                self.copyf(i, e).wait_send()
        for e in range(1, 8):
            self.copyz(e).wait_send()


def exchange_scratch():
    dma = pltpu.SemaphoreType.DMA
    pairs = [(NCH, 16), (NCH, 8), (NCH, 8), (8,), (NCH, 8), (NCH, 16)]
    return [
        pltpu.VMEM((8, CG, 2 * LR, LW), BF16),
        pltpu.VMEM((SG, CG, 64, 128), BF16),
        pltpu.VMEM((SG, CG, 64, 128), BF16),
        pltpu.VMEM((NX, 2, CG, 2, 16, 128), BF16),
        pltpu.VMEM((8, CG, 2, 16, 128), BF16),
        pltpu.VMEM((BS * 32, 128), F32),
        pltpu.VMEM((8, CG, 2, 16, 128), BF16),
        pltpu.VMEM((NX, CG, 2, 32, 128), BF16),
        pltpu.VMEM((SG, CG, 64, 128), BF16),
        pltpu.VMEM((SG, CG, 64, 128), BF16),
        pltpu.VMEM((8, CG, 2 * LR, LW), BF16),
    ] + [dma(shape) for shape in pairs for _ in range(2)]


class Reduction:
    def __init__(self, ex, scratch):
        self.ex = ex
        self.src, self.ra, self.t1, self.rb, self.t2, self.rc, self.out = scratch[:7]
        self.sems = scratch[7:17]

    def copy_a(self):
        ex = self.ex
        return pltpu.make_async_remote_copy(
            src_ref=self.src.at[1 - ex.core],
            dst_ref=self.ra,
            send_sem=self.sems[0],
            recv_sem=self.sems[1],
            device_id=(2 * ex.s + 1 - ex.core, ex.ci),
            device_id_type=MESH,
        )

    def copy_b(self, e):
        ex = self.ex
        s = (ex.s + e) % SG
        return pltpu.make_async_remote_copy(
            src_ref=self.t1.at[s],
            dst_ref=self.rb.at[ex.s],
            send_sem=self.sems[2].at[e],
            recv_sem=self.sems[3].at[e],
            device_id=(2 * s + ex.core, ex.ci),
            device_id_type=MESH,
        )

    def copy_c(self, e):
        ex = self.ex
        return pltpu.make_async_remote_copy(
            src_ref=self.t2,
            dst_ref=self.rc.at[ex.ci],
            send_sem=self.sems[4].at[e],
            recv_sem=self.sems[5].at[e],
            device_id=(ex.ri, (ex.ci + e) % 8),
            device_id_type=MESH,
        )

    def copy_d(self, e):
        ex = self.ex
        return pltpu.make_async_remote_copy(
            src_ref=self.out.at[ex.core, ex.s],
            dst_ref=self.out.at[ex.core, ex.s],
            send_sem=self.sems[6].at[e],
            recv_sem=self.sems[7].at[e],
            device_id=(2 * ((ex.s + e) % SG) + ex.core, ex.ci),
            device_id_type=MESH,
        )

    def copy_e(self):
        ex = self.ex
        return pltpu.make_async_remote_copy(
            src_ref=self.out.at[ex.core],
            dst_ref=self.out.at[ex.core],
            send_sem=self.sems[8],
            recv_sem=self.sems[9],
            device_id=(2 * ex.s + 1 - ex.core, ex.ci),
            device_id_type=MESH,
        )

    def round(self, number):
        ex = self.ex
        if number == 0:
            self.copy_a().start()
        elif number == 1:
            self.copy_a().wait_recv()
            self.t1[...] = self.src[ex.core] + self.ra[...]
            for e in range(1, 8):
                self.copy_b(e).start()
            self.rb[ex.s] = self.t1[ex.s]
        elif number == 2:
            for e in range(1, 8):
                self.copy_b(e).wait_recv()
            self.t2[...] = jnp.sum(self.rb[...], axis=0)
            for e in range(1, 8):
                self.copy_c(e).start()
            self.rc[ex.ci] = self.t2[...]
        elif number == 3:
            for e in range(1, 8):
                self.copy_c(e).wait_recv()
            self.out[ex.core, ex.s] = jnp.sum(self.rc[...], axis=0) * (1.0 / H)
            for e in range(1, 8):
                self.copy_d(e).start()
        elif number == 4:
            for e in range(1, 8):
                self.copy_d(e).wait_recv()
            self.copy_e().start()
        else:
            self.copy_e().wait_recv()
            self.copy_a().wait_send()
            self.copy_e().wait_send()
            for e in range(1, 8):
                self.copy_b(e).wait_send()
                self.copy_c(e).wait_send()
                self.copy_d(e).wait_send()


def reduction_scratch(rows, lanes, source):
    dma = pltpu.SemaphoreType.DMA
    part = pltpu.VMEM((8, rows, lanes), F32)
    buffers = [pltpu.VMEM((2, 8, rows, lanes), F32)] if source else []
    return (
        buffers
        + [part, part, part, pltpu.VMEM((rows, lanes), F32), part, pltpu.VMEM((2, 8, rows, lanes), F32)]
        + [dma] * 2
        + [dma((8,))] * 6
        + [dma] * 2
    )


def channel_mean(read):
    total = read(0)
    for c in range(1, C):
        total = total + read(c)
    return total * (1.0 / C)


def norm_rows(field, rows):
    mean = channel_mean(lambda c: field[c, rows, :].astype(F32))

    def square(c):
        centred = field[c, rows, :].astype(F32) - mean
        return centred * centred

    return mean, lax.rsqrt(channel_mean(square) + EPS)


def forward_kernel(
    weather, width, weighted, height, spectral_in, bias, spectral_out,
    normed, filtered, kept, before_out, hidden_out, slope_out, *scratch
):
    ex = Exchange(scratch)

    @pl.loop(0, LR // 16)
    def _(r):
        rows = pl.ds(pl.multiple_of(r * 16, 16), 16)
        mean, spread = norm_rows(weather, rows)
        for c in range(C):
            normed[c, rows, :] = ((weather[c, rows, :].astype(F32) - mean) * spread).astype(BF16)

    ex.barrier()
    ex.send1(normed)
    ex.width_forward(normed, width)
    ex.height_forward(height)
    ex.modes(kept)

    a_re, a_im = spectral_in[0, ex.yh], spectral_in[1, ex.yh]
    b_re, b_im = spectral_out[0, ex.yh], spectral_out[1, ex.yh]

    def mixed(lo, hi):
        real, imaginary = kept[:BS, lo:hi], kept[BS:, lo:hi]
        before = jnp.concatenate(
            [
                dot_tn(a_re, real) - dot_tn(a_im, imaginary) + bias[0, ex.yh],
                dot_tn(a_re, imaginary) + dot_tn(a_im, real) + bias[1, ex.yh],
            ],
            axis=0,
        )
        before_out[:, lo:hi] = before
        cumulative, _ = normal_parts(before)
        hidden = (before * cumulative).astype(BF16)
        hidden_out[:, lo:hi] = hidden
        real, imaginary = hidden[:BS], hidden[BS:]
        second = jnp.concatenate(
            [
                dot_tn(b_re, real) - dot_tn(b_im, imaginary),
                dot_tn(b_re, imaginary) + dot_tn(b_im, real),
            ],
            axis=0,
        )
        slope = jnp.tanh(second * (1.0 / THRESHOLD))
        slope_out[:, lo:hi] = slope
        return second - THRESHOLD * slope

    ex.from_modes(mixed)
    ex.height_inverse(height)
    ex.width_inverse(filtered, weighted)
    ex.finish(normed, filtered)


def backward_kernel(
    weather, grad_sum, token_grads, width, weighted, height, spectral_in, spectral_out,
    kept, before, hidden, slope,
    grad_weather, grad_pin, grad_pout, grad_in, grad_out, grad_bias,
    low, filtered, grads, gate, *scratch
):
    ex = Exchange(scratch)
    first = Reduction(ex, (token_grads,) + scratch[23:39])
    other = Reduction(ex, scratch[39:56])

    @pl.loop(0, LR // 16)
    def _(r):
        rows = pl.ds(pl.multiple_of(r * 16, 16), 16)
        for c in range(C):
            low[c, rows, :] = grad_sum[c, rows, :].astype(BF16)

    ex.barrier()
    first.round(0)
    ex.send1(low)
    ex.width_forward(low, weighted)
    first.round(1)
    ex.height_forward(height)
    first.round(2)
    ex.modes(grads)
    a_re, a_im = spectral_in[0, ex.yh], spectral_in[1, ex.yh]
    b_re, b_im = spectral_out[0, ex.yh], spectral_out[1, ex.yh]

    def mixed(lo, hi):
        factor = slope[:, lo:hi]
        second = (grads[:, lo:hi].astype(F32) * (factor * factor)).astype(BF16)
        grads[:, lo:hi] = second
        real, imaginary = second[:BS], second[BS:]
        back = jnp.concatenate(
            [
                dot_nn(b_re, real) + dot_nn(b_im, imaginary),
                dot_nn(b_re, imaginary) - dot_nn(b_im, real),
            ],
            axis=0,
        )
        values = before[:, lo:hi]
        cumulative, density = normal_parts(values)
        gated = (back * (cumulative + values * density)).astype(BF16)
        gate[:, lo:hi] = gated
        real, imaginary = gated[:BS], gated[BS:]
        return jnp.concatenate(
            [
                dot_nn(a_re, real) + dot_nn(a_im, imaginary),
                dot_nn(a_re, imaginary) - dot_nn(a_im, real),
            ],
            axis=0,
        )

    ex.from_modes(mixed)
    first.round(3)
    sums = other.src
    sums[...] = jnp.zeros_like(sums)
    low_half, high_half = slice(0, BS), slice(BS, 2 * BS)
    for base, left, right in ((0, kept, gate), (2, hidden, grads)):
        real = dot_nt(left[low_half, :], right[low_half, :]) + dot_nt(
            left[high_half, :], right[high_half, :]
        )
        imaginary = dot_nt(left[low_half, :], right[high_half, :]) - dot_nt(
            left[high_half, :], right[low_half, :]
        )
        for part, value in enumerate((real, imaginary)):
            at = 2 * (base + part)
            sums[ex.yh, at : at + 2, :, :BS] = value.reshape(2, 48, BS)
    for part in range(2):
        value = jnp.sum(gate[part * BS : (part + 1) * BS, :].astype(F32), axis=1, keepdims=True)
        sums[ex.yh, 2 * part : 2 * part + 2, :, BS : BS + 1] = value.reshape(2, 48, 1)
    other.round(0)
    ex.height_inverse(height)
    first.round(4)
    other.round(1)
    ex.width_inverse(filtered, width)
    other.round(2)
    first.round(5)
    other.round(3)
    grad_pin[...] = first.out[0].reshape(C, HID)
    grad_pout[...] = first.out[1].reshape(C, HID).T
    other.round(4)
    ex.finish(low, filtered)
    other.round(5)
    for block in range(2):
        for part in range(2):
            for base, target in ((0, grad_in), (2, grad_out)):
                at = 2 * (base + part)
                target[part, block] = other.out[block, at : at + 2, :, :BS].reshape(BS, BS)
            grad_bias[part, block] = other.out[block, 2 * part : 2 * part + 2, :, BS : BS + 1].reshape(BS, 1)

    @pl.loop(0, LR // 16)
    def _(r):
        rows = pl.ds(pl.multiple_of(r * 16, 16), 16)
        mean, spread = norm_rows(weather, rows)

        def total(c):
            return grad_sum[c, rows, :] + filtered[c, rows, :].astype(F32)

        def normal(c):
            return (weather[c, rows, :].astype(F32) - mean) * spread

        mean_grad = channel_mean(total)
        mean_cross = channel_mean(lambda c: total(c) * normal(c))
        for c in range(C):
            inner = total(c) - mean_grad - normal(c) * mean_cross
            grad_weather[c, rows, :] = (grad_sum[c, rows, :] + spread * inner).astype(BF16)


TR = 16
TN = TR * LW
CHUNK = 512


def token_kernel(
    weather, normed_in, filtered, cotangent, pin, pout,
    output, grad_sum, grads, acc_in, acc_out, pin_t, pout_t, s32, x32, c32, g32, normal_low, cot_low
):
    step = pl.program_id(0)

    @pl.when(step == 0)
    def _():
        acc_in[...] = jnp.zeros_like(acc_in)
        acc_out[...] = jnp.zeros_like(acc_out)
        pin_t[...] = pin[...].T
        pout_t[...] = pout[...].T

    def at(c):
        return slice(c * TR, (c + 1) * TR)

    total = jnp.zeros((TR, LW), F32)
    for c in range(C):
        value = weather[c].astype(F32) + normed_in[c].astype(F32) + filtered[c].astype(F32)
        s32[at(c), :] = value
        total = total + value
        c32[at(c), :] = cotangent[c].astype(F32)
    mean = total * (1.0 / C)

    def square(c):
        centred = s32[at(c), :] - mean
        return centred * centred

    spread = lax.rsqrt(channel_mean(square) + EPS)
    for c in range(C):
        x32[at(c), :] = (s32[at(c), :] - mean) * spread
    for j in range(TR):
        lanes = slice(j * LW, (j + 1) * LW)
        normal_low[:, lanes] = x32[pl.ds(j, C, stride=TR), :].astype(BF16)
        cot_low[:, lanes] = c32[pl.ds(j, C, stride=TR), :].astype(BF16)

    @pl.loop(0, TN // CHUNK)
    def _(q):
        lanes = pl.ds(pl.multiple_of(q * CHUNK, CHUNK), CHUNK)
        normal = normal_low[:, lanes]
        cot = cot_low[:, lanes]
        before = dot_nn(pin_t[...], normal)
        cumulative, density = normal_parts(before)
        hidden = (before * cumulative).astype(BF16)
        back_hidden = dot_nn(pout[...], cot)
        back_before = (back_hidden * (cumulative + before * density)).astype(BF16)
        out = dot_nn(pout_t[...], hidden)
        back_normed = dot_nn(pin[...], back_before)
        acc_out[...] += dot_nt(hidden, cot)
        acc_in[...] += dot_nt(back_before, normal)
        for j in range(CHUNK // LW):
            sl = slice(j * LW, (j + 1) * LW)
            where = pl.ds(q * (CHUNK // LW) + j, C, stride=TR)
            s32[where, :] += out[:, sl]
            g32[where, :] = back_normed[:, sl]

    for c in range(C):
        output[c] = s32[at(c), :].astype(BF16)
    mean_grad = channel_mean(lambda c: g32[at(c), :])
    mean_cross = channel_mean(lambda c: g32[at(c), :] * x32[at(c), :])
    for c in range(C):
        inner = g32[at(c), :] - mean_grad - x32[at(c), :] * mean_cross
        grad_sum[c] = c32[at(c), :] + spread * inner

    @pl.when(step == pl.num_programs(0) - 1)
    def _():
        grads[0] = acc_in[...].T.reshape(8, 24, HID)
        grads[1] = acc_out[...].T.reshape(8, 24, HID)


def vmem():
    return pl.BlockSpec(memory_space=pltpu.VMEM)


def forward_call(*args):
    shape = jax.ShapeDtypeStruct
    return pl.pallas_call(
        forward_kernel,
        out_shape=(
            shape((C, LR, LW), BF16),
            shape((C, LR, LW), BF16),
            shape((C, MODES), BF16),
            shape((C, MODES), F32),
            shape((C, MODES), BF16),
            shape((C, MODES), F32),
        ),
        in_specs=[vmem()] * 7,
        out_specs=[vmem()] * 6,
        scratch_shapes=exchange_scratch(),
        compiler_params=pltpu.CompilerParams(
            collective_id=0, has_side_effects=True, vmem_limit_bytes=60 << 20
        ),
        name="spectral_forward",
    )(*args)


def backward_call(*args):
    shape = jax.ShapeDtypeStruct
    return pl.pallas_call(
        backward_kernel,
        out_shape=(
            shape((C, LR, LW), BF16),
            shape((C, HID), F32),
            shape((HID, C), F32),
            shape((2, NB, BS, BS), F32),
            shape((2, NB, BS, BS), F32),
            shape((2, NB, BS, 1), F32),
        ),
        in_specs=[vmem()] * 12,
        out_specs=[vmem()] * 6,
        scratch_shapes=[
            pltpu.VMEM((C, LR, LW), BF16),
            pltpu.VMEM((C, LR, LW), BF16),
            pltpu.VMEM((C, MODES), BF16),
            pltpu.VMEM((C, MODES), BF16),
        ]
        + exchange_scratch()
        + reduction_scratch(24, HID, False)
        + reduction_scratch(48, 128, True),
        compiler_params=pltpu.CompilerParams(
            collective_id=1, has_side_effects=True, vmem_limit_bytes=63 << 20
        ),
        name="spectral_backward",
    )(*args)


def token_call(*args):
    shape = jax.ShapeDtypeStruct
    block = pl.BlockSpec((C, TR, LW), lambda i: (0, i, 0))

    def whole(*dims):
        return pl.BlockSpec(dims, lambda i: (0,) * len(dims))

    return pl.pallas_call(
        token_kernel,
        grid=(LR // TR,),
        out_shape=(
            shape((C, LR, LW), BF16),
            shape((C, LR, LW), F32),
            shape((2, 8, 24, HID), F32),
        ),
        in_specs=[block] * 4 + [whole(C, HID), whole(HID, C)],
        out_specs=[block, block, whole(2, 8, 24, HID)],
        scratch_shapes=[pltpu.VMEM((HID, C), F32)] * 2
        + [pltpu.VMEM((HID, C), BF16), pltpu.VMEM((C, HID), BF16)]
        + [pltpu.VMEM((C * TR, LW), F32)] * 4
        + [pltpu.VMEM((C, TN), BF16)] * 2,
        compiler_params=pltpu.CompilerParams(vmem_limit_bytes=60 << 20),
        name="token_block",
    )(*args)


def body(weather, cotangent, spectral_in, spectral_bias, spectral_out, project_in, project_out):
    width, weighted, height = tables()
    bias = spectral_bias.reshape(2, NB, BS, 1)
    normed, filtered, kept, before, hidden, slope = forward_call(
        weather, width, weighted, height, spectral_in, bias, spectral_out
    )
    output, grad_sum, token_grads = token_call(
        weather, normed, filtered, cotangent, project_in, project_out
    )
    grad_weather, grad_pin, grad_pout, grad_in, grad_out, grad_bias = backward_call(
        weather, grad_sum, token_grads, width, weighted, height, spectral_in, spectral_out,
        kept, before, hidden, slope,
    )
    return (
        output,
        grad_weather,
        grad_pin,
        grad_pout,
        grad_in,
        grad_out,
        grad_bias.reshape(2, NB, BS),
    )


def solution(mesh):
    in_specs = (P(None, "row", "col"), P(None, "row", "col"), P(), P(), P(), P(), P())
    out_specs = (P(None, "row", "col"), P(None, "row", "col"), P(), P(), P(), P(), P())
    return jax.shard_map(body, mesh=mesh, in_specs=in_specs, out_specs=out_specs, check_vma=False)
```

```python
from functools import partial
import math

import numpy as np
import jax
import jax.numpy as jnp
from jax import lax
from jax.experimental import pallas as pl
from jax.experimental.pallas import tpu as pltpu
from jax.sharding import PartitionSpec as P

H = 1024
W = 1024
NB = 2
BS = 96
C = 192
HID = 768
KH = 512
KW = 256

LR = 64
LW = 128
CG = 12
CH = 4
NCH = CG // CH
NX = 4
SG = 8
MODES = 2048
TR = 16
RB = LR // TR
TN = TR * LW
CHUNK = 512
EPS = 1e-05
THRESHOLD = 0.1
F32 = jnp.float32
BF16 = jnp.bfloat16
MESH = pl.DeviceIdType.MESH


def tables():
    k = np.arange(KW)
    angle = (k[:, None] * np.arange(W)[None, :] % W).astype(np.float32) * np.float32(2.0 * math.pi / W)
    factor = np.float32(1.0 / math.sqrt(W))
    cosine, sine = np.cos(angle) * factor, -np.sin(angle) * factor
    width = np.stack([cosine.reshape(SG, 32, W), sine.reshape(SG, 32, W)], axis=1).reshape(2 * KW, W)
    weight = np.where(k == 0, 1.0, 2.0).astype(np.float32)[:, None]
    weighted = np.stack(
        [(cosine * weight).reshape(SG, 32, W), (sine * weight).reshape(SG, 32, W)], axis=1
    ).reshape(2 * KW, W)
    m = np.arange(KH)
    frequency = np.where(m < KH // 2, m, m + (H - KH))
    angle = (np.arange(H)[:, None] * frequency[None, :] % H).astype(np.float32) * np.float32(
        2.0 * math.pi / H
    )
    factor = np.float32(1.0 / math.sqrt(H))
    height = np.concatenate([np.cos(angle) * factor, -np.sin(angle) * factor], axis=1)
    return tuple(jnp.asarray(t, F32).astype(BF16) for t in (width, weighted, height))


def dot_nn(left, right):
    return lax.dot_general(left, right, (((1,), (0,)), ((), ())), preferred_element_type=F32)


def dot_nt(left, right):
    return lax.dot_general(left, right, (((1,), (1,)), ((), ())), preferred_element_type=F32)


def dot_tn(left, right):
    return lax.dot_general(left, right, (((0,), (0,)), ((), ())), preferred_element_type=F32)


def normal_parts(values):
    cumulative = 0.5 * (1.0 + lax.erf(values * (1.0 / math.sqrt(2.0))))
    density = jnp.exp(-0.5 * values * values) * (1.0 / math.sqrt(2.0 * math.pi))
    return cumulative, density


class Exchange:
    def __init__(self, buffers, sems):
        (self.X, self.O, self.G, self.K, self.Y0, self.y32, self.Z0, self.Q, self.BK, self.F, self.FO) = buffers
        self.sems = sems
        self.ri = lax.axis_index("row")
        self.ci = lax.axis_index("col")
        self.core = self.ri % 2
        self.s = self.ri // 2
        self.x = self.ci // 2
        self.yh = self.ci % 2
        self.id1 = self.ci * 2 + self.core
        self.id2 = self.x * 2 + self.core

    def peer1(self, d):
        other = (self.id1 + d) % 16
        return other // 2, other % 2

    def peer2(self, e):
        other = (self.id2 + e) % 8
        return other // 2, other % 2

    def barrier(self):
        sem = pltpu.get_barrier_semaphore()
        for d in range(1, 16):
            col, core = self.peer1(d)
            pl.semaphore_signal(sem, inc=1, device_id=(2 * self.s + core, col), device_id_type=MESH)
        for e in range(1, SG):
            s = (self.s + e) % SG
            pl.semaphore_signal(sem, inc=1, device_id=(2 * s + self.core, self.ci), device_id_type=MESH)
        pl.semaphore_wait(sem, 15 + SG - 1)

    def first_channel(self, col, core):
        return (col % 2) * BS + (col // 2) * (2 * CG) + core * CG

    def copy1(self, src, i, d):
        col, core = self.peer1(d)
        start = self.first_channel(col, core) + i * CH
        rows = pl.ds(pl.multiple_of(self.core * LR, LR), LR)
        return pltpu.make_async_remote_copy(
            src_ref=src.at[pl.ds(start, CH)],
            dst_ref=self.X.at[self.ci, pl.ds(i * CH, CH), rows, :],
            send_sem=self.sems[0].at[i, d],
            recv_sem=self.sems[1].at[i, d],
            device_id=(2 * self.s + core, col),
            device_id_type=MESH,
        )

    def rows1(self, src, r, d):
        col, core = self.peer1(d)
        rows = pl.ds(pl.multiple_of(r * TR, TR), TR)
        there = pl.ds(pl.multiple_of(self.core * LR + r * TR, TR), TR)
        return pltpu.make_async_remote_copy(
            src_ref=src.at[pl.ds(self.first_channel(col, core), CG), rows, :],
            dst_ref=self.X.at[self.ci, :, there, :],
            send_sem=self.sems[0].at[r, d],
            recv_sem=self.sems[1].at[r, d],
            device_id=(2 * self.s + core, col),
            device_id_type=MESH,
        )

    def send_rows1(self, src, r):
        rows = pl.ds(pl.multiple_of(r * TR, TR), TR)
        there = pl.ds(pl.multiple_of(self.core * LR + r * TR, TR), TR)
        own = self.first_channel(self.ci, self.core)
        for d in range(1, 16):
            self.rows1(src, r, d).start()
        self.X[self.ci, :, there, :] = src[pl.ds(own, CG), rows, :]

    def send1(self, src):
        rows = pl.ds(pl.multiple_of(self.core * LR, LR), LR)
        own = self.first_channel(self.ci, self.core)
        for i in range(NCH):
            for d in range(1, 16):
                self.copy1(src, i, d).start()
        self.X[self.ci, :, rows, :] = src[pl.ds(own, CG)]

    def copyb(self, i, e):
        s = (self.s + e) % SG
        return pltpu.make_async_remote_copy(
            src_ref=self.O.at[s, pl.ds(i * CH, CH)],
            dst_ref=self.G.at[self.s, pl.ds(i * CH, CH)],
            send_sem=self.sems[2].at[i, e],
            recv_sem=self.sems[3].at[i, e],
            device_id=(2 * s + self.core, self.ci),
            device_id_type=MESH,
        )

    def width_forward(self, src, table, by_rows):
        if by_rows:

            @pl.loop(0, RB)
            def _(r):
                for d in range(1, 16):
                    self.rows1(src, r, d).wait_recv()

        @pl.loop(0, NCH)
        def _(i):
            if not by_rows:
                for d in range(1, 16):
                    self.copy1(src, i, d).wait_recv()
            for half in range(CH // 2):
                c = i * CH + 2 * half
                field = jnp.concatenate(
                    [self.X[p, pl.ds(c, 2)].reshape(2 * 2 * LR, LW) for p in range(8)], axis=1
                )
                spectrum = dot_nt(table[...], field).astype(BF16)
                for j in range(2):
                    self.O[:, c + j] = spectrum[:, j * 128 : (j + 1) * 128].reshape(SG, 64, 128)
            for e in range(1, SG):
                self.copyb(i, e).start()
            own = pl.ds(i * CH, CH)
            self.G[self.s, own] = self.O[self.s, own]

    def copyc(self, i, e):
        x, core = self.peer2(e)
        return pltpu.make_async_remote_copy(
            src_ref=self.K.at[x, core, pl.ds(i * CH, CH)],
            dst_ref=self.Y0.at[self.id2, pl.ds(i * CH, CH)],
            send_sem=self.sems[4].at[i, e],
            recv_sem=self.sems[5].at[i, e],
            device_id=(2 * self.s + core, 2 * x + self.yh),
            device_id_type=MESH,
        )

    def height_forward(self, table):
        @pl.loop(0, NCH)
        def _(i):
            for e in range(1, SG):
                self.copyb(i, e).wait_recv()
            own = pl.ds(i * CH, CH)
            spectrum = jnp.concatenate(
                [self.G[s, own].reshape(CH * 64, 128) for s in range(SG)], axis=1
            )
            for x in range(NX):
                lanes = slice(x * 128, (x + 1) * 128)
                shifted = slice(KH + x * 128, KH + (x + 1) * 128)
                both = jnp.concatenate([table[:, lanes], table[:, shifted]], axis=1)
                terms = dot_nn(spectrum, both).reshape(CH, 2, 2, 16, 256)
                real = terms[:, 0, :, :, :128] - terms[:, 1, :, :, 128:]
                imaginary = terms[:, 0, :, :, 128:] + terms[:, 1, :, :, :128]
                for core in range(2):
                    self.K[x, core, own, 0] = real[:, core].astype(BF16)
                    self.K[x, core, own, 1] = imaginary[:, core].astype(BF16)
            for e in range(1, 8):
                self.copyc(i, e).start()
            self.Y0[self.id2, own] = self.K[self.x, self.core, own]

    def modes(self, out):
        @pl.loop(0, NCH)
        def _(i):
            for e in range(1, 8):
                self.copyc(i, e).wait_recv()
        self.y32[...] = self.Y0[...].astype(F32).reshape(BS * 32, 128)
        for part in range(2):
            for k in range(16):
                out[part * BS : (part + 1) * BS, k * 128 : (k + 1) * 128] = self.y32[
                    pl.ds(part * 16 + k, BS, stride=32), :
                ].astype(BF16)

    def copyz(self, i, e):
        x, core = self.peer2(e)
        return pltpu.make_async_remote_copy(
            src_ref=self.Z0.at[x * 2 + core, pl.ds(i * CH, CH)],
            dst_ref=self.Q.at[self.x, pl.ds(i * CH, CH), :, pl.ds(pl.multiple_of(self.core * 16, 16), 16), :],
            send_sem=self.sems[6].at[i, e],
            recv_sem=self.sems[7].at[i, e],
            device_id=(2 * self.s + core, 2 * x + self.yh),
            device_id_type=MESH,
        )

    def from_modes(self, values):
        for q in range(4):
            block = values(q * 512, (q + 1) * 512)
            for part in range(2):
                for j in range(4):
                    self.y32[pl.ds(part * 16 + q * 4 + j, BS, stride=32), :] = block[
                        part * BS : (part + 1) * BS, j * 128 : (j + 1) * 128
                    ]
        self.Z0[...] = self.y32[...].astype(BF16).reshape(8, CG, 2, 16, 128)
        for i in range(NCH):
            for e in range(1, 8):
                self.copyz(i, e).start()
        self.Q[self.x, :, :, pl.ds(pl.multiple_of(self.core * 16, 16), 16), :] = self.Z0[self.id2]

    def copyf(self, i, e):
        s = (self.s + e) % SG
        return pltpu.make_async_remote_copy(
            src_ref=self.BK.at[s, pl.ds(i * CH, CH)],
            dst_ref=self.F.at[self.s, pl.ds(i * CH, CH)],
            send_sem=self.sems[8].at[i, e],
            recv_sem=self.sems[9].at[i, e],
            device_id=(2 * s + self.core, self.ci),
            device_id_type=MESH,
        )

    def height_inverse(self, table):
        @pl.loop(0, NCH)
        def _(i):
            for e in range(1, 8):
                self.copyz(i, e).wait_recv()
            own = pl.ds(i * CH, CH)
            modes = jnp.concatenate([self.Q[x, own].reshape(CH * 64, 128) for x in range(NX)], axis=1)
            for q in range(4):
                rows = slice(q * 256, (q + 1) * 256)
                first = dot_nt(modes, table[rows, :KH]).reshape(CH, 2, 32, 256)
                second = dot_nt(modes, table[rows, KH:]).reshape(CH, 2, 32, 256)
                real = (first[:, 0] + second[:, 1]).astype(BF16)
                imaginary = (first[:, 1] - second[:, 0]).astype(BF16)
                for j in range(2):
                    lanes = slice(j * 128, (j + 1) * 128)
                    self.BK[2 * q + j, own, :32, :] = real[:, :, lanes]
                    self.BK[2 * q + j, own, 32:, :] = imaginary[:, :, lanes]
            for e in range(1, SG):
                self.copyf(i, e).start()
            self.F[self.s, own] = self.BK[self.s, own]

    def copyo(self, out, i, d):
        col, core = self.peer1(d)
        start = self.first_channel(self.ci, self.core) + i * CH
        rows = pl.ds(pl.multiple_of(core * LR, LR), LR)
        return pltpu.make_async_remote_copy(
            src_ref=self.FO.at[col, pl.ds(i * CH, CH), rows, :],
            dst_ref=out.at[pl.ds(start, CH)],
            send_sem=self.sems[10].at[i, d],
            recv_sem=self.sems[11].at[i, d],
            device_id=(2 * self.s + core, col),
            device_id_type=MESH,
        )

    def rowso(self, out, r, d):
        col, core = self.peer1(d)
        rows = pl.ds(pl.multiple_of(core * LR + r * TR, TR), TR)
        there = pl.ds(pl.multiple_of(r * TR, TR), TR)
        return pltpu.make_async_remote_copy(
            src_ref=self.FO.at[col, :, rows, :],
            dst_ref=out.at[pl.ds(self.first_channel(self.ci, self.core), CG), there, :],
            send_sem=self.sems[10].at[r, d],
            recv_sem=self.sems[11].at[r, d],
            device_id=(2 * self.s + core, col),
            device_id_type=MESH,
        )

    def width_inverse(self, out, table, by_rows):
        rows = pl.ds(pl.multiple_of(self.core * LR, LR), LR)
        start = self.first_channel(self.ci, self.core)

        @pl.loop(0, NCH)
        def _(i):
            for e in range(1, SG):
                self.copyf(i, e).wait_recv()
            for half in range(CH // 2):
                c = i * CH + 2 * half
                spectrum = jnp.concatenate(
                    [self.F[:, c].reshape(2 * KW, 128), self.F[:, c + 1].reshape(2 * KW, 128)], axis=1
                )
                turned = spectrum.T
                for q in range(4):
                    field = dot_nn(turned, table[:, q * 256 : (q + 1) * 256]).astype(BF16)
                    for j in range(2):
                        self.FO[2 * q + j, pl.ds(c, 2)] = field[:, j * 128 : (j + 1) * 128].reshape(
                            2, 128, 128
                        )
            if not by_rows:
                for d in range(1, 16):
                    self.copyo(out, i, d).start()
            out[pl.ds(start + i * CH, CH)] = self.FO[self.ci, pl.ds(i * CH, CH), rows, :]

        if by_rows:

            @pl.loop(0, RB)
            def _(r):
                for d in range(1, 16):
                    self.rowso(out, r, d).start()

    def drain(self, src, first):
        @pl.loop(0, RB if first else NCH)
        def _(i):
            for d in range(1, 16):
                (self.rows1 if first else self.copy1)(src, i, d).wait_send()

        @pl.loop(0, NCH)
        def _(i):
            for e in range(1, 8):
                self.copyb(i, e).wait_send()
                self.copyc(i, e).wait_send()
                self.copyz(i, e).wait_send()
                self.copyf(i, e).wait_send()

    def drain_out(self, out, by_rows):
        @pl.loop(0, RB if by_rows else NCH)
        def _(i):
            for d in range(1, 16):
                (self.rowso if by_rows else self.copyo)(out, i, d).wait_send()


def exchange_scratch():
    return [
        pltpu.VMEM((8, CG, 2 * LR, LW), BF16),
        pltpu.VMEM((SG, CG, 64, 128), BF16),
        pltpu.VMEM((SG, CG, 64, 128), BF16),
        pltpu.VMEM((NX, 2, CG, 2, 16, 128), BF16),
        pltpu.VMEM((8, CG, 2, 16, 128), BF16),
        pltpu.VMEM((BS * 32, 128), F32),
        pltpu.VMEM((8, CG, 2, 16, 128), BF16),
        pltpu.VMEM((NX, CG, 2, 32, 128), BF16),
        pltpu.VMEM((SG, CG, 64, 128), BF16),
        pltpu.VMEM((SG, CG, 64, 128), BF16),
        pltpu.VMEM((8, CG, 2 * LR, LW), BF16),
    ]


def exchange_semaphores():
    most = max(NCH, RB)
    pairs = [(most, 16), (NCH, 8), (NCH, 8), (NCH, 8), (NCH, 8), (most, 16)]
    return [pltpu.SemaphoreType.DMA(shape) for shape in pairs for _ in range(2)]


class Reduction:
    def __init__(self, ex, scratch):
        self.ex = ex
        self.src, self.ra, self.t1, self.rb, self.t2, self.rc, self.out = scratch[:7]
        self.sems = scratch[7:17]

    def copy_a(self):
        ex = self.ex
        return pltpu.make_async_remote_copy(
            src_ref=self.src.at[1 - ex.core],
            dst_ref=self.ra,
            send_sem=self.sems[0],
            recv_sem=self.sems[1],
            device_id=(2 * ex.s + 1 - ex.core, ex.ci),
            device_id_type=MESH,
        )

    def copy_b(self, e):
        ex = self.ex
        s = (ex.s + e) % SG
        return pltpu.make_async_remote_copy(
            src_ref=self.t1.at[s],
            dst_ref=self.rb.at[ex.s],
            send_sem=self.sems[2].at[e],
            recv_sem=self.sems[3].at[e],
            device_id=(2 * s + ex.core, ex.ci),
            device_id_type=MESH,
        )

    def copy_c(self, e):
        ex = self.ex
        return pltpu.make_async_remote_copy(
            src_ref=self.t2,
            dst_ref=self.rc.at[ex.ci],
            send_sem=self.sems[4].at[e],
            recv_sem=self.sems[5].at[e],
            device_id=(ex.ri, (ex.ci + e) % 8),
            device_id_type=MESH,
        )

    def copy_d(self, e):
        ex = self.ex
        return pltpu.make_async_remote_copy(
            src_ref=self.out.at[ex.core, ex.s],
            dst_ref=self.out.at[ex.core, ex.s],
            send_sem=self.sems[6].at[e],
            recv_sem=self.sems[7].at[e],
            device_id=(2 * ((ex.s + e) % SG) + ex.core, ex.ci),
            device_id_type=MESH,
        )

    def copy_e(self):
        ex = self.ex
        return pltpu.make_async_remote_copy(
            src_ref=self.out.at[ex.core],
            dst_ref=self.out.at[ex.core],
            send_sem=self.sems[8],
            recv_sem=self.sems[9],
            device_id=(2 * ex.s + 1 - ex.core, ex.ci),
            device_id_type=MESH,
        )

    def round(self, number):
        ex = self.ex
        if number == 0:
            self.copy_a().start()
        elif number == 1:
            self.copy_a().wait_recv()
            self.t1[...] = self.src[ex.core] + self.ra[...]
            for e in range(1, 8):
                self.copy_b(e).start()
            self.rb[ex.s] = self.t1[ex.s]
        elif number == 2:
            for e in range(1, 8):
                self.copy_b(e).wait_recv()
            self.t2[...] = jnp.sum(self.rb[...], axis=0)
            for e in range(1, 8):
                self.copy_c(e).start()
            self.rc[ex.ci] = self.t2[...]
        elif number == 3:
            for e in range(1, 8):
                self.copy_c(e).wait_recv()
            self.out[ex.core, ex.s] = jnp.sum(self.rc[...], axis=0) * (1.0 / H)
            for e in range(1, 8):
                self.copy_d(e).start()
        elif number == 4:
            for e in range(1, 8):
                self.copy_d(e).wait_recv()
            self.copy_e().start()
        else:
            self.copy_e().wait_recv()
            self.copy_a().wait_send()
            self.copy_e().wait_send()
            for e in range(1, 8):
                self.copy_b(e).wait_send()
                self.copy_c(e).wait_send()
                self.copy_d(e).wait_send()


def reduction_scratch(rows, lanes):
    dma = pltpu.SemaphoreType.DMA
    part = pltpu.VMEM((8, rows, lanes), F32)
    return (
        [pltpu.VMEM((2, 8, rows, lanes), F32)]
        + [part, part, part, pltpu.VMEM((rows, lanes), F32), part, pltpu.VMEM((2, 8, rows, lanes), F32)]
        + [dma] * 2
        + [dma((8,))] * 6
        + [dma] * 2
    )


def channel_mean(read):
    total = read(0)
    for c in range(1, C):
        total = total + read(c)
    return total * (1.0 / C)


def token_rows(r, weather, normed, filtered, cot, pin, pin_t, pout, pout_t, acc_in, acc_out,
               s32, x32, gc, normal_low, cot_low, output, out_copy, sum_copy, next_cot):
    rows = pl.ds(pl.multiple_of(r * TR, TR), TR)
    g32, c32 = gc.at[0], gc.at[1]

    def at(c):
        return slice(c * TR, (c + 1) * TR)

    total = jnp.zeros((TR, LW), F32)
    for c in range(C):
        value = (
            weather[c, rows, :].astype(F32)
            + normed[c, rows, :].astype(F32)
            + filtered[c, rows, :].astype(F32)
        )
        s32[at(c), :] = value
        total = total + value
        c32[at(c), :] = cot[c].astype(F32)

    @pl.when(r < RB - 1)
    def _():
        next_cot(r + 1).start()

    mean = total * (1.0 / C)

    def square(c):
        centred = s32[at(c), :] - mean
        return centred * centred

    spread = lax.rsqrt(channel_mean(square) + EPS)
    for c in range(C):
        x32[at(c), :] = (s32[at(c), :] - mean) * spread
    for j in range(TR):
        lanes = slice(j * LW, (j + 1) * LW)
        normal_low[:, lanes] = x32[pl.ds(j, C, stride=TR), :].astype(BF16)
        cot_low[:, lanes] = c32[pl.ds(j, C, stride=TR), :].astype(BF16)

    @pl.when(r > 0)
    def _():
        sum_copy(r).wait()
        out_copy(r).wait()

    @pl.loop(0, TN // CHUNK)
    def _(q):
        lanes = pl.ds(pl.multiple_of(q * CHUNK, CHUNK), CHUNK)
        normal = normal_low[:, lanes]
        cot_now = cot_low[:, lanes]
        before = dot_nn(pin_t[...], normal)
        cumulative, density = normal_parts(before)
        hidden = (before * cumulative).astype(BF16)
        back_hidden = dot_nn(pout[...], cot_now)
        back_before = (back_hidden * (cumulative + before * density)).astype(BF16)
        out = dot_nn(pout_t[...], hidden)
        back_normed = dot_nn(pin[...], back_before)
        acc_out[...] += dot_nt(hidden, cot_now)
        acc_in[...] += dot_nt(back_before, normal)
        for j in range(CHUNK // LW):
            sl = slice(j * LW, (j + 1) * LW)
            where = pl.ds(q * (CHUNK // LW) + j, C, stride=TR)
            s32[where, :] += out[:, sl]
            g32[where, :] = back_normed[:, sl]

    for c in range(C):
        output[c] = s32[at(c), :].astype(BF16)
    out_copy(r).start()
    mean_grad = channel_mean(lambda c: g32[at(c), :])
    mean_cross = channel_mean(lambda c: g32[at(c), :] * x32[at(c), :])
    for c in range(C):
        inner = g32[at(c), :] - mean_grad - x32[at(c), :] * mean_cross
        value = c32[at(c), :] + spread * inner
        g32[at(c), :] = value
        normed[c, rows, :] = value.astype(BF16)
    sum_copy(r).start()


def mix_forward(ex, kept, before_all, hidden_all, slope_all, spectral_in, bias, spectral_out):
    a_re, a_im = spectral_in[0, ex.yh], spectral_in[1, ex.yh]
    b_re, b_im = spectral_out[0, ex.yh], spectral_out[1, ex.yh]
    bias_re, bias_im = (
        jnp.broadcast_to(bias[part, pl.ds(ex.yh, 1), :], (BS, BS)).T[:, :1] for part in range(2)
    )

    def mixed(lo, hi):
        real, imaginary = kept[:BS, lo:hi], kept[BS:, lo:hi]
        before = jnp.concatenate(
            [
                dot_tn(a_re, real) - dot_tn(a_im, imaginary) + bias_re,
                dot_tn(a_re, imaginary) + dot_tn(a_im, real) + bias_im,
            ],
            axis=0,
        )
        before_all[:, lo:hi] = before
        cumulative, _ = normal_parts(before)
        hidden = (before * cumulative).astype(BF16)
        hidden_all[:, lo:hi] = hidden
        real, imaginary = hidden[:BS], hidden[BS:]
        second = jnp.concatenate(
            [
                dot_tn(b_re, real) - dot_tn(b_im, imaginary),
                dot_tn(b_re, imaginary) + dot_tn(b_im, real),
            ],
            axis=0,
        )
        slope = jnp.tanh(second * (1.0 / THRESHOLD))
        slope_all[:, lo:hi] = slope
        return second - THRESHOLD * slope

    ex.from_modes(mixed)


def mix_backward(ex, grads, gate, before, slope, spectral_in, spectral_out):
    a_re, a_im = spectral_in[0, ex.yh], spectral_in[1, ex.yh]
    b_re, b_im = spectral_out[0, ex.yh], spectral_out[1, ex.yh]

    def mixed(lo, hi):
        factor = slope[:, lo:hi]
        second = (grads[:, lo:hi].astype(F32) * (factor * factor)).astype(BF16)
        grads[:, lo:hi] = second
        real, imaginary = second[:BS], second[BS:]
        back = jnp.concatenate(
            [
                dot_nn(b_re, real) + dot_nn(b_im, imaginary),
                dot_nn(b_re, imaginary) - dot_nn(b_im, real),
            ],
            axis=0,
        )
        values = before[:, lo:hi]
        cumulative, density = normal_parts(values)
        gated = (back * (cumulative + values * density)).astype(BF16)
        gate[:, lo:hi] = gated
        real, imaginary = gated[:BS], gated[BS:]
        return jnp.concatenate(
            [
                dot_nn(a_re, real) + dot_nn(a_im, imaginary),
                dot_nn(a_re, imaginary) - dot_nn(a_im, real),
            ],
            axis=0,
        )

    ex.from_modes(mixed)


def spectral_sums(ex, sums, kept, gate, hidden, grads):
    sums[...] = jnp.zeros_like(sums)
    low_half, high_half = slice(0, BS), slice(BS, 2 * BS)
    for base, left, right in ((0, kept, gate), (2, hidden, grads)):
        real = dot_nt(left[low_half, :], right[low_half, :]) + dot_nt(
            left[high_half, :], right[high_half, :]
        )
        imaginary = dot_nt(left[low_half, :], right[high_half, :]) - dot_nt(
            left[high_half, :], right[low_half, :]
        )
        for part, value in enumerate((real, imaginary)):
            at = 2 * (base + part)
            sums[ex.yh, at : at + 2, :, :BS] = value.reshape(2, 48, BS)
    for part in range(2):
        value = jnp.sum(gate[part * BS : (part + 1) * BS, :].astype(F32), axis=1, keepdims=True)
        sums[ex.yh, 2 * part : 2 * part + 2, :, BS : BS + 1] = value.reshape(2, 48, 1)


def layer_kernel(
    weather, cotangent, width, weighted, height, spectral_in, bias, spectral_out, pin, pout_t,
    output, grad_weather, grad_pin, grad_pout_t, grad_in, grad_out, grad_bias, sum_hbm, *scratch
):
    (normed, filtered, stats, cot, out_block, kept, before, hidden, slope, grads, gate,
     acc_in, acc_out, pin_t, pout, x32, gc, normal_low, cot_low, cot_sem, out_sem, sum_sem) = scratch[:22]
    scratch = scratch[22:]
    buffers, scratch = scratch[:11], scratch[11:]
    ex = Exchange(buffers, scratch[:12])
    back = Exchange(buffers, scratch[12:24])
    first = Reduction(ex, scratch[24:41])
    other = Reduction(ex, scratch[41:58])
    s32 = ex.y32

    def rows_of(r):
        return pl.ds(pl.multiple_of(r * TR, TR), TR)

    def next_cot(r):
        return pltpu.make_async_copy(cotangent.at[:, rows_of(r), :], cot, cot_sem)

    def out_copy(r):
        return pltpu.make_async_copy(out_block, output.at[:, rows_of(r), :], out_sem)

    def sum_copy(r):
        return pltpu.make_async_copy(gc.at[0], sum_hbm.at[r], sum_sem)

    def grad_copy(r):
        return pltpu.make_async_copy(out_block, grad_weather.at[:, rows_of(r), :], out_sem)

    next_cot(0).start()

    @pl.loop(0, RB)
    def _(r):
        rows = rows_of(r)
        mean = channel_mean(lambda c: weather[c, rows, :].astype(F32))

        def square(c):
            centred = weather[c, rows, :].astype(F32) - mean
            return centred * centred

        spread = lax.rsqrt(channel_mean(square) + EPS)
        stats[0, rows, :] = mean
        stats[1, rows, :] = spread
        for c in range(C):
            normed[c, rows, :] = ((weather[c, rows, :].astype(F32) - mean) * spread).astype(BF16)

    ex.barrier()
    ex.send1(normed)
    pin_t[...] = pin[...].T
    pout[...] = pout_t[...].T
    acc_in[...] = jnp.zeros_like(acc_in)
    acc_out[...] = jnp.zeros_like(acc_out)
    ex.width_forward(normed, width, False)
    ex.height_forward(height)
    ex.modes(kept)
    mix_forward(ex, kept, before, hidden, slope, spectral_in, bias, spectral_out)
    ex.height_inverse(height)
    ex.width_inverse(filtered, weighted, True)
    ex.drain(normed, False)

    @pl.loop(0, RB)
    def _(r):
        for d in range(1, 16):
            ex.rowso(filtered, r, d).wait_recv()
        next_cot(r).wait()
        token_rows(
            r, weather, normed, filtered, cot, pin, pin_t, pout, pout_t, acc_in, acc_out,
            s32, x32, gc, normal_low, cot_low, out_block, out_copy, sum_copy, next_cot,
        )
        back.send_rows1(normed, r)

    first.src[0] = acc_in[...].T.reshape(8, 24, HID)
    first.src[1] = acc_out[...].T.reshape(8, 24, HID)
    first.round(0)
    sum_copy(0).wait()
    out_copy(0).wait()
    ex.drain_out(filtered, True)
    back.width_forward(normed, weighted, True)
    first.round(1)
    back.height_forward(height)
    first.round(2)
    back.modes(grads)
    mix_backward(back, grads, gate, before, slope, spectral_in, spectral_out)
    first.round(3)
    spectral_sums(back, other.src, kept, gate, hidden, grads)
    other.round(0)
    back.height_inverse(height)
    first.round(4)
    other.round(1)
    back.width_inverse(filtered, width, False)
    other.round(2)
    first.round(5)
    other.round(3)
    grad_pin[...] = first.out[0].reshape(C, HID)
    grad_pout_t[...] = first.out[1].reshape(C, HID)
    other.round(4)

    def sum_back(r, slot):
        return pltpu.make_async_copy(sum_hbm.at[r], gc.at[slot], sum_sem)

    sum_back(0, 0).start()

    @pl.loop(0, NCH)
    def _(i):
        for d in range(1, 16):
            back.copyo(filtered, i, d).wait_recv()

    @pl.loop(0, RB)
    def _(r):
        rows = rows_of(r)
        slot = r % 2
        sum_back(r, slot).wait()

        @pl.when(r < RB - 1)
        def _():
            sum_back(r + 1, 1 - slot).start()

        mean = stats[0, rows, :]
        spread = stats[1, rows, :]

        def own(c):
            return gc[slot, pl.ds(c * TR, TR), :]

        def total(c):
            return own(c) + filtered[c, rows, :].astype(F32)

        def normal(c):
            return (weather[c, rows, :].astype(F32) - mean) * spread

        mean_grad = channel_mean(total)
        mean_cross = channel_mean(lambda c: total(c) * normal(c))

        @pl.when(r > 0)
        def _():
            grad_copy(r).wait()

        for c in range(C):
            inner = total(c) - mean_grad - normal(c) * mean_cross
            out_block[c] = (own(c) + spread * inner).astype(BF16)
        grad_copy(r).start()

    other.round(5)
    for block in range(2):
        for part in range(2):
            for base, target in ((0, grad_in), (2, grad_out)):
                at = 2 * (base + part)
                target[part, block] = other.out[block, at : at + 2, :, :BS].reshape(BS, BS)
            column = other.out[block, 2 * part : 2 * part + 2, :, BS : BS + 1].reshape(BS, 1)
            grad_bias[part, block : block + 1, :] = jnp.broadcast_to(column, (BS, BS)).T[:1, :]
    back.drain(normed, True)
    back.drain_out(filtered, False)
    grad_copy(0).wait()


def layer_call(*args):
    shape = jax.ShapeDtypeStruct
    dma = pltpu.SemaphoreType.DMA
    vmem, anywhere = (pl.BlockSpec(memory_space=space) for space in (pltpu.VMEM, pl.ANY))
    return pl.pallas_call(
        layer_kernel,
        out_shape=(
            shape((C, LR, LW), BF16),
            shape((C, LR, LW), BF16),
            shape((C, HID), F32),
            shape((C, HID), F32),
            shape((2, NB, BS, BS), F32),
            shape((2, NB, BS, BS), F32),
            shape((2, NB, BS), F32),
            shape((RB, C * TR, LW), F32),
        ),
        in_specs=[vmem, anywhere] + [vmem] * 8,
        out_specs=[anywhere, anywhere] + [vmem] * 5 + [anywhere],
        scratch_shapes=[
            pltpu.VMEM((C, LR, LW), BF16),
            pltpu.VMEM((C, LR, LW), BF16),
            pltpu.VMEM((2, LR, LW), F32),
            pltpu.VMEM((C, TR, LW), BF16),
            pltpu.VMEM((C, TR, LW), BF16),
            pltpu.VMEM((C, MODES), BF16),
            pltpu.VMEM((C, MODES), F32),
            pltpu.VMEM((C, MODES), BF16),
            pltpu.VMEM((C, MODES), F32),
            pltpu.VMEM((C, MODES), BF16),
            pltpu.VMEM((C, MODES), BF16),
            pltpu.VMEM((HID, C), F32),
            pltpu.VMEM((HID, C), F32),
            pltpu.VMEM((HID, C), BF16),
            pltpu.VMEM((HID, C), BF16),
            pltpu.VMEM((C * TR, LW), F32),
            pltpu.VMEM((2, C * TR, LW), F32),
            pltpu.VMEM((C, TN), BF16),
            pltpu.VMEM((C, TN), BF16),
            dma,
            dma,
            dma,
        ]
        + exchange_scratch()
        + exchange_semaphores()
        + exchange_semaphores()
        + reduction_scratch(24, HID)
        + reduction_scratch(48, 128),
        compiler_params=pltpu.CompilerParams(
            collective_id=0, has_side_effects=True, vmem_limit_bytes=67043328
        ),
        name="layer",
    )(*args)


def body(weather, cotangent, spectral_in, spectral_bias, spectral_out, project_in, project_out):
    width, weighted, height = tables()
    output, grad_weather, grad_pin, grad_pout_t, grad_in, grad_out, grad_bias, _ = layer_call(
        weather, cotangent, width, weighted, height, spectral_in, spectral_bias, spectral_out,
        project_in, project_out.T,
    )
    return output, grad_weather, grad_pin, grad_pout_t.T, grad_in, grad_out, grad_bias


def solution(mesh):
    in_specs = (P(None, "row", "col"), P(None, "row", "col"), P(), P(), P(), P(), P())
    out_specs = (P(None, "row", "col"), P(None, "row", "col"), P(), P(), P(), P(), P())
    return jax.shard_map(body, mesh=mesh, in_specs=in_specs, out_specs=out_specs, check_vma=False)
```

```python
from functools import partial
import math

import numpy as np
import jax
import jax.numpy as jnp
from jax import lax
from jax.experimental import pallas as pl
from jax.experimental.pallas import tpu as pltpu
from jax.sharding import PartitionSpec as P

H = 1024
W = 1024
NB = 2
BS = 96
C = 192
HID = 768
KH = 512
KW = 256

LR = 64
LW = 128
CG = 12
CH = 2
NCH = CG // CH
NX = 4
SG = 8
MODES = 2048
TR = 16
RB = LR // TR
TN = TR * LW
CHUNK = 512
EPS = 1e-05
THRESHOLD = 0.1
F32 = jnp.float32
BF16 = jnp.bfloat16
MESH = pl.DeviceIdType.MESH


def tables():
    k = np.arange(KW)
    angle = (k[:, None] * np.arange(W)[None, :] % W).astype(np.float32) * np.float32(2.0 * math.pi / W)
    factor = np.float32(1.0 / math.sqrt(W))
    cosine, sine = np.cos(angle) * factor, -np.sin(angle) * factor
    width = np.stack([cosine.reshape(SG, 32, W), sine.reshape(SG, 32, W)], axis=1).reshape(2 * KW, W)
    weight = np.where(k == 0, 1.0, 2.0).astype(np.float32)[:, None]
    weighted = np.stack(
        [(cosine * weight).reshape(SG, 32, W), (sine * weight).reshape(SG, 32, W)], axis=1
    ).reshape(2 * KW, W)
    m = np.arange(KH)
    frequency = np.where(m < KH // 2, m, m + (H - KH))
    angle = (np.arange(H)[:, None] * frequency[None, :] % H).astype(np.float32) * np.float32(
        2.0 * math.pi / H
    )
    factor = np.float32(1.0 / math.sqrt(H))
    height = np.concatenate([np.cos(angle) * factor, -np.sin(angle) * factor], axis=1)
    return tuple(jnp.asarray(t, F32).astype(BF16) for t in (width, weighted, height))


def dot_nn(left, right):
    return lax.dot_general(left, right, (((1,), (0,)), ((), ())), preferred_element_type=F32)


def dot_nt(left, right):
    return lax.dot_general(left, right, (((1,), (1,)), ((), ())), preferred_element_type=F32)


def dot_tn(left, right):
    return lax.dot_general(left, right, (((0,), (0,)), ((), ())), preferred_element_type=F32)


def normal_parts(values):
    cumulative = 0.5 * (1.0 + lax.erf(values * (1.0 / math.sqrt(2.0))))
    density = jnp.exp(-0.5 * values * values) * (1.0 / math.sqrt(2.0 * math.pi))
    return cumulative, density


class Exchange:
    def __init__(self, buffers, sems):
        (self.X, self.O, self.G, self.K, self.Y0, self.y32, self.Z0, self.Q, self.BK, self.F, self.FO) = buffers
        self.sems = sems
        self.ri = lax.axis_index("row")
        self.ci = lax.axis_index("col")
        self.core = self.ri % 2
        self.s = self.ri // 2
        self.x = self.ci // 2
        self.yh = self.ci % 2
        self.id1 = self.ci * 2 + self.core
        self.id2 = self.x * 2 + self.core
        self.z = self.s % 4
        self.id3 = (self.s // 4) * 8 + self.ci

    def peer1(self, d):
        other = (self.id1 + d) % 16
        return other // 2, other % 2

    def peer2(self, e):
        other = (self.id2 + e) % 8
        return other // 2, other % 2

    def peer3(self, d):
        other = (self.id3 + d) % 16
        return other // 8, other % 8

    def greet(self):
        sem = pltpu.get_barrier_semaphore()
        for d in range(1, 16):
            col, core = self.peer1(d)
            pl.semaphore_signal(sem, inc=1, device_id=(2 * self.s + core, col), device_id_type=MESH)
        for e in range(1, SG):
            s = (self.s + e) % SG
            pl.semaphore_signal(sem, inc=1, device_id=(2 * s + self.core, self.ci), device_id_type=MESH)
        other_lo = 1 - self.s // 4
        for e in range(1, 8):
            row = 2 * (4 * other_lo + self.z) + self.core
            pl.semaphore_signal(sem, inc=1, device_id=(row, (self.ci + e) % 8), device_id_type=MESH)

    def barrier(self):
        pl.semaphore_wait(pltpu.get_barrier_semaphore(), 15 + SG - 1 + 7)

    def first_channel(self, col, core):
        return (col % 2) * BS + (col // 2) * (2 * CG) + core * CG

    def copy1(self, src, i, d):
        col, core = self.peer1(d)
        start = self.first_channel(col, core) + i * CH
        rows = pl.ds(pl.multiple_of(self.core * LR, LR), LR)
        return pltpu.make_async_remote_copy(
            src_ref=src.at[pl.ds(start, CH)],
            dst_ref=self.X.at[self.ci, pl.ds(i * CH, CH), rows, :],
            send_sem=self.sems[0].at[i, d],
            recv_sem=self.sems[1].at[i, d],
            device_id=(2 * self.s + core, col),
            device_id_type=MESH,
        )

    def rows1(self, src, r, d):
        col, core = self.peer1(d)
        rows = pl.ds(pl.multiple_of(r * TR, TR), TR)
        there = pl.ds(pl.multiple_of(self.core * LR + r * TR, TR), TR)
        return pltpu.make_async_remote_copy(
            src_ref=src.at[pl.ds(self.first_channel(col, core), CG), rows, :],
            dst_ref=self.X.at[self.ci, :, there, :],
            send_sem=self.sems[0].at[r, d],
            recv_sem=self.sems[1].at[r, d],
            device_id=(2 * self.s + core, col),
            device_id_type=MESH,
        )

    def send_rows1(self, src, r):
        rows = pl.ds(pl.multiple_of(r * TR, TR), TR)
        there = pl.ds(pl.multiple_of(self.core * LR + r * TR, TR), TR)
        own = self.first_channel(self.ci, self.core)
        for d in range(1, 16):
            self.rows1(src, r, d).start()
        self.X[self.ci, :, there, :] = src[pl.ds(own, CG), rows, :]

    def send1(self, src):
        rows = pl.ds(pl.multiple_of(self.core * LR, LR), LR)
        own = self.first_channel(self.ci, self.core)
        for i in range(NCH):
            for d in range(1, 16):
                self.copy1(src, i, d).start()
        self.X[self.ci, :, rows, :] = src[pl.ds(own, CG)]

    def copyb(self, i, e):
        s = (self.s + e) % SG
        return pltpu.make_async_remote_copy(
            src_ref=self.O.at[s, pl.ds(i * CH, CH)],
            dst_ref=self.G.at[self.s, pl.ds(i * CH, CH)],
            send_sem=self.sems[2].at[i, e],
            recv_sem=self.sems[3].at[i, e],
            device_id=(2 * s + self.core, self.ci),
            device_id_type=MESH,
        )

    def width_forward(self, src, table, by_rows):
        if by_rows:

            @pl.loop(0, RB)
            def _(r):
                for d in range(1, 16):
                    self.rows1(src, r, d).wait_recv()

        @pl.loop(0, NCH)
        def _(i):
            if not by_rows:
                for d in range(1, 16):
                    self.copy1(src, i, d).wait_recv()
            for half in range(CH // 2):
                c = i * CH + 2 * half
                field = jnp.concatenate(
                    [self.X[p, pl.ds(c, 2)].reshape(2 * 2 * LR, LW) for p in range(8)], axis=1
                )
                spectrum = dot_nt(table[...], field).astype(BF16)
                for j in range(2):
                    self.O[:, c + j] = spectrum[:, j * 128 : (j + 1) * 128].reshape(SG, 64, 128)
            for e in range(1, SG):
                self.copyb(i, e).start()
            own = pl.ds(i * CH, CH)
            self.G[self.s, own] = self.O[self.s, own]

    def copyc(self, i, e):
        x, core = self.peer2(e)
        return pltpu.make_async_remote_copy(
            src_ref=self.K.at[x, core, pl.ds(i * CH, CH)],
            dst_ref=self.Y0.at[self.id2, pl.ds(i * CH, CH)],
            send_sem=self.sems[4].at[i, e],
            recv_sem=self.sems[5].at[i, e],
            device_id=(2 * self.s + core, 2 * x + self.yh),
            device_id_type=MESH,
        )

    def height_forward(self, table):
        @pl.loop(0, NCH)
        def _(i):
            for e in range(1, SG):
                self.copyb(i, e).wait_recv()
            own = pl.ds(i * CH, CH)
            spectrum = jnp.concatenate(
                [self.G[s, own].reshape(CH * 64, 128) for s in range(SG)], axis=1
            )
            for x in range(NX):
                lanes = slice(x * 128, (x + 1) * 128)
                shifted = slice(KH + x * 128, KH + (x + 1) * 128)
                both = jnp.concatenate([table[:, lanes], table[:, shifted]], axis=1)
                terms = dot_nn(spectrum, both).reshape(CH, 2, 2, 16, 256)
                real = terms[:, 0, :, :, :128] - terms[:, 1, :, :, 128:]
                imaginary = terms[:, 0, :, :, 128:] + terms[:, 1, :, :, :128]
                for core in range(2):
                    self.K[x, core, own, 0] = real[:, core].astype(BF16)
                    self.K[x, core, own, 1] = imaginary[:, core].astype(BF16)
            for e in range(1, 8):
                self.copyc(i, e).start()
            self.Y0[self.id2, own] = self.K[self.x, self.core, own]

    def modes(self, out):
        @pl.loop(0, NCH)
        def _(i):
            for e in range(1, 8):
                self.copyc(i, e).wait_recv()
        self.y32[...] = self.Y0[...].astype(F32).reshape(BS * 32, 128)
        for part in range(2):
            for k in range(16):
                out[part * BS : (part + 1) * BS, k * 128 : (k + 1) * 128] = self.y32[
                    pl.ds(part * 16 + k, BS, stride=32), :
                ].astype(BF16)

    def copyz(self, i, e):
        x, core = self.peer2(e)
        return pltpu.make_async_remote_copy(
            src_ref=self.Z0.at[x * 2 + core, pl.ds(i * CH, CH)],
            dst_ref=self.Q.at[self.x, pl.ds(i * CH, CH), :, pl.ds(pl.multiple_of(self.core * 16, 16), 16), :],
            send_sem=self.sems[6].at[i, e],
            recv_sem=self.sems[7].at[i, e],
            device_id=(2 * self.s + core, 2 * x + self.yh),
            device_id_type=MESH,
        )

    def from_modes(self, values):
        for q in range(4):
            block = values(q * 512, (q + 1) * 512)
            for part in range(2):
                for j in range(4):
                    self.y32[pl.ds(part * 16 + q * 4 + j, BS, stride=32), :] = block[
                        part * BS : (part + 1) * BS, j * 128 : (j + 1) * 128
                    ]
        self.Z0[...] = self.y32[...].astype(BF16).reshape(8, CG, 2, 16, 128)
        for i in range(NCH):
            for e in range(1, 8):
                self.copyz(i, e).start()
        self.Q[self.x, :, :, pl.ds(pl.multiple_of(self.core * 16, 16), 16), :] = self.Z0[self.id2]

    def copyf(self, i, e):
        s = (self.s + e) % SG
        return pltpu.make_async_remote_copy(
            src_ref=self.BK.at[s, pl.ds(i * CH, CH)],
            dst_ref=self.F.at[self.s, pl.ds(i * CH, CH)],
            send_sem=self.sems[8].at[i, e],
            recv_sem=self.sems[9].at[i, e],
            device_id=(2 * s + self.core, self.ci),
            device_id_type=MESH,
        )

    def height_inverse(self, table):
        @pl.loop(0, NCH)
        def _(i):
            for e in range(1, 8):
                self.copyz(i, e).wait_recv()
            own = pl.ds(i * CH, CH)
            modes = jnp.concatenate([self.Q[x, own].reshape(CH * 64, 128) for x in range(NX)], axis=1)
            for q in range(4):
                rows = slice(q * 256, (q + 1) * 256)
                first = dot_nt(modes, table[rows, :KH]).reshape(CH, 2, 32, 256)
                second = dot_nt(modes, table[rows, KH:]).reshape(CH, 2, 32, 256)
                real = (first[:, 0] + second[:, 1]).astype(BF16)
                imaginary = (first[:, 1] - second[:, 0]).astype(BF16)
                for j in range(2):
                    lanes = slice(j * 128, (j + 1) * 128)
                    self.BK[2 * q + j, own, :32, :] = real[:, :, lanes]
                    self.BK[2 * q + j, own, 32:, :] = imaginary[:, :, lanes]
            for e in range(1, SG):
                self.copyf(i, e).start()
            self.F[self.s, own] = self.BK[self.s, own]

    def copyo(self, out, i, d):
        col, core = self.peer1(d)
        start = self.first_channel(self.ci, self.core) + i * CH
        rows = pl.ds(pl.multiple_of(core * LR, LR), LR)
        return pltpu.make_async_remote_copy(
            src_ref=self.FO.at[col, pl.ds(i * CH, CH), rows, :],
            dst_ref=out.at[pl.ds(start, CH)],
            send_sem=self.sems[10].at[i, d],
            recv_sem=self.sems[11].at[i, d],
            device_id=(2 * self.s + core, col),
            device_id_type=MESH,
        )

    def rowso(self, out, r, d):
        col, core = self.peer1(d)
        rows = pl.ds(pl.multiple_of(core * LR + r * TR, TR), TR)
        there = pl.ds(pl.multiple_of(r * TR, TR), TR)
        return pltpu.make_async_remote_copy(
            src_ref=self.FO.at[col, :, rows, :],
            dst_ref=out.at[pl.ds(self.first_channel(self.ci, self.core), CG), there, :],
            send_sem=self.sems[10].at[r, d],
            recv_sem=self.sems[11].at[r, d],
            device_id=(2 * self.s + core, col),
            device_id_type=MESH,
        )

    def width_inverse(self, out, table, by_rows):
        rows = pl.ds(pl.multiple_of(self.core * LR, LR), LR)
        start = self.first_channel(self.ci, self.core)

        @pl.loop(0, NCH)
        def _(i):
            for e in range(1, SG):
                self.copyf(i, e).wait_recv()
            for half in range(CH // 2):
                c = i * CH + 2 * half
                spectrum = jnp.concatenate(
                    [self.F[:, c].reshape(2 * KW, 128), self.F[:, c + 1].reshape(2 * KW, 128)], axis=1
                )
                turned = spectrum.T
                for q in range(4):
                    field = dot_nn(turned, table[:, q * 256 : (q + 1) * 256]).astype(BF16)
                    for j in range(2):
                        self.FO[2 * q + j, pl.ds(c, 2)] = field[:, j * 128 : (j + 1) * 128].reshape(
                            2, 128, 128
                        )
            if not by_rows:
                for d in range(1, 16):
                    self.copyo(out, i, d).start()
            out[pl.ds(start + i * CH, CH)] = self.FO[self.ci, pl.ds(i * CH, CH), rows, :]

        if by_rows:

            @pl.loop(0, RB)
            def _(r):
                for d in range(1, 16):
                    self.rowso(out, r, d).start()

    def drain(self, src, first):
        @pl.loop(0, RB if first else NCH)
        def _(i):
            for d in range(1, 16):
                (self.rows1 if first else self.copy1)(src, i, d).wait_send()

        @pl.loop(0, NCH)
        def _(i):
            for e in range(1, 8):
                self.copyb(i, e).wait_send()
                self.copyc(i, e).wait_send()
                self.copyz(i, e).wait_send()
                self.copyf(i, e).wait_send()

    def drain_out(self, out, by_rows):
        @pl.loop(0, RB if by_rows else NCH)
        def _(i):
            for d in range(1, 16):
                (self.rowso if by_rows else self.copyo)(out, i, d).wait_send()


def exchange_scratch():
    return [
        pltpu.VMEM((8, CG, 2 * LR, LW), BF16),
        pltpu.VMEM((SG, CG, 64, 128), BF16),
        pltpu.VMEM((SG, CG, 64, 128), BF16),
        pltpu.VMEM((NX, 2, CG, 2, 16, 128), BF16),
        pltpu.VMEM((8, CG, 2, 16, 128), BF16),
        pltpu.VMEM((BS * 32, 128), F32),
        pltpu.VMEM((8, CG, 2, 16, 128), BF16),
        pltpu.VMEM((NX, CG, 2, 32, 128), BF16),
        pltpu.VMEM((SG, CG, 64, 128), BF16),
        pltpu.VMEM((SG, CG, 64, 128), BF16),
        pltpu.VMEM((8, CG, 2 * LR, LW), BF16),
    ]


def exchange_semaphores():
    most = max(NCH, RB)
    pairs = [(most, 16), (NCH, 8), (NCH, 8), (NCH, 8), (NCH, 8), (most, 16)]
    return [pltpu.SemaphoreType.DMA(shape) for shape in pairs for _ in range(2)]


class Reduction:
    def __init__(self, ex, scratch, n):
        self.ex = ex
        self.n = n
        self.src, self.ra, self.t1, self.rb, self.t2, self.rc, self.out = scratch[:7]
        self.sems = scratch[7:19]

    def copy_a(self, dst, src, k):
        ex = self.ex
        return pltpu.make_async_remote_copy(
            src_ref=src,
            dst_ref=dst,
            send_sem=self.sems[k],
            recv_sem=self.sems[k + 1],
            device_id=(2 * ex.s + 1 - ex.core, ex.ci),
            device_id_type=MESH,
        )

    def first_core(self):
        return self.copy_a(self.ra, self.src.at[1 - self.ex.core], 0)

    def last_core(self):
        own = self.out.at[self.ex.core]
        return self.copy_a(own, own, 10)

    def over_z(self, dst, src, k, e):
        ex = self.ex
        return pltpu.make_async_remote_copy(
            src_ref=src,
            dst_ref=dst,
            send_sem=self.sems[k].at[e],
            recv_sem=self.sems[k + 1].at[e],
            device_id=(2 * ((ex.s // 4) * 4 + (ex.z + e) % 4) + ex.core, ex.ci),
            device_id_type=MESH,
        )

    def first_z(self, e):
        return self.over_z(self.rb.at[self.ex.z], self.t1.at[(self.ex.z + e) % 4], 2, e)

    def last_z(self, e):
        own = self.out.at[self.ex.core, self.ex.z]
        return self.over_z(own, own, 8, e)

    def over_rest(self, dst, src, k, d):
        ex = self.ex
        low, col = ex.peer3(d)
        return pltpu.make_async_remote_copy(
            src_ref=src,
            dst_ref=dst,
            send_sem=self.sems[k].at[d],
            recv_sem=self.sems[k + 1].at[d],
            device_id=(2 * (low * 4 + ex.z) + ex.core, col),
            device_id_type=MESH,
        )

    def guard(self, member, action):
        pl.when(member < self.n)(action)

    def peer(self, d):
        return (self.ex.id3 + d) % 16

    def piece_at(self, member):
        return lax.min(member, self.n - 1)

    def first_rest(self, d):
        return self.over_rest(self.rc.at[self.ex.id3], self.t2.at[self.piece_at(self.peer(d))], 4, d)

    def last_rest(self, d, member):
        own = self.out.at[self.ex.core, self.ex.z, self.piece_at(member)]
        return self.over_rest(own, own, 6, d)

    def round(self, number):
        ex = self.ex
        if number == 0:
            self.first_core().start()
        elif number == 1:
            self.first_core().wait_recv()
            self.t1[...] = self.src[ex.core] + self.ra[...]
            for e in range(1, 4):
                self.first_z(e).start()
            self.rb[ex.z] = self.t1[ex.z]
        elif number == 2:
            for e in range(1, 4):
                self.first_z(e).wait_recv()
            self.t2[...] = self.rb[0] + self.rb[1] + self.rb[2] + self.rb[3]
            for d in range(1, 16):
                self.guard(self.peer(d), lambda d=d: self.first_rest(d).start())
            self.guard(ex.id3, self.keep)
        elif number == 3:
            self.guard(ex.id3, self.add)
        elif number == 4:
            for d in range(1, 16):
                source = (ex.id3 + 16 - d) % 16
                self.guard(source, lambda d=d, source=source: self.last_rest(d, source).wait_recv())
            for e in range(1, 4):
                self.last_z(e).start()
        elif number == 5:
            for e in range(1, 4):
                self.last_z(e).wait_recv()
            self.last_core().start()
        else:
            self.last_core().wait_recv()
            self.first_core().wait_send()
            self.last_core().wait_send()
            for e in range(1, 4):
                self.first_z(e).wait_send()
                self.last_z(e).wait_send()
            for d in range(1, 16):
                self.guard(self.peer(d), lambda d=d: self.first_rest(d).wait_send())
            self.guard(ex.id3, self.sent)

    def keep(self):
        self.rc[self.ex.id3] = self.t2[self.piece_at(self.ex.id3)]

    def add(self):
        ex = self.ex
        for d in range(1, 16):
            self.first_rest(d).wait_recv()
        total = self.rc[0]
        for member in range(1, 16):
            total = total + self.rc[member]
        self.out[ex.core, ex.z, self.piece_at(ex.id3)] = total * (1.0 / H)
        for d in range(1, 16):
            self.last_rest(d, ex.id3).start()

    def sent(self):
        for d in range(1, 16):
            self.last_rest(d, self.ex.id3).wait_send()


def reduction_scratch(n):
    dma = pltpu.SemaphoreType.DMA
    part = pltpu.VMEM((4, n, 24, 128), F32)
    whole = pltpu.VMEM((2, 4, n, 24, 128), F32)
    return (
        [whole, part, part, part, pltpu.VMEM((n, 24, 128), F32), pltpu.VMEM((16, 24, 128), F32), whole]
        + [dma] * 2
        + [dma((4,))] * 2
        + [dma((16,))] * 4
        + [dma((4,))] * 2
        + [dma] * 2
    )


def channel_mean(read):
    total = read(0)
    for c in range(1, C):
        total = total + read(c)
    return total * (1.0 / C)


def token_rows(r, weather, normed, filtered, cot, pin, pin_t, pout, pout_t, acc_in, acc_out,
               s32, x32, gc, normal_low, cot_low, output, out_copy, sum_copy, next_cot):
    rows = pl.ds(pl.multiple_of(r * TR, TR), TR)
    g32, c32 = gc.at[0], gc.at[1]

    def at(c):
        return slice(c * TR, (c + 1) * TR)

    total = jnp.zeros((TR, LW), F32)
    for c in range(C):
        value = (
            weather[c, rows, :].astype(F32)
            + normed[c, rows, :].astype(F32)
            + filtered[c, rows, :].astype(F32)
        )
        s32[at(c), :] = value
        total = total + value
        c32[at(c), :] = cot[c].astype(F32)

    @pl.when(r < RB - 1)
    def _():
        next_cot(r + 1).start()

    mean = total * (1.0 / C)

    def square(c):
        centred = s32[at(c), :] - mean
        return centred * centred

    spread = lax.rsqrt(channel_mean(square) + EPS)
    for c in range(C):
        x32[at(c), :] = (s32[at(c), :] - mean) * spread
    for j in range(TR):
        lanes = slice(j * LW, (j + 1) * LW)
        normal_low[:, lanes] = x32[pl.ds(j, C, stride=TR), :].astype(BF16)
        cot_low[:, lanes] = c32[pl.ds(j, C, stride=TR), :].astype(BF16)

    @pl.when(r > 0)
    def _():
        sum_copy(r).wait()
        out_copy(r).wait()

    @pl.loop(0, TN // CHUNK)
    def _(q):
        lanes = pl.ds(pl.multiple_of(q * CHUNK, CHUNK), CHUNK)
        normal = normal_low[:, lanes]
        cot_now = cot_low[:, lanes]
        before = dot_nn(pin_t[...], normal)
        cumulative, density = normal_parts(before)
        hidden = (before * cumulative).astype(BF16)
        back_hidden = dot_nn(pout[...], cot_now)
        back_before = (back_hidden * (cumulative + before * density)).astype(BF16)
        out = dot_nn(pout_t[...], hidden)
        back_normed = dot_nn(pin[...], back_before)
        acc_out[...] += dot_nt(hidden, cot_now)
        acc_in[...] += dot_nt(back_before, normal)
        for j in range(CHUNK // LW):
            sl = slice(j * LW, (j + 1) * LW)
            where = pl.ds(q * (CHUNK // LW) + j, C, stride=TR)
            s32[where, :] += out[:, sl]
            g32[where, :] = back_normed[:, sl]

    for c in range(C):
        output[c] = s32[at(c), :].astype(BF16)
    out_copy(r).start()
    mean_grad = channel_mean(lambda c: g32[at(c), :])
    mean_cross = channel_mean(lambda c: g32[at(c), :] * x32[at(c), :])
    for c in range(C):
        inner = g32[at(c), :] - mean_grad - x32[at(c), :] * mean_cross
        value = c32[at(c), :] + spread * inner
        g32[at(c), :] = value
        normed[c, rows, :] = value.astype(BF16)
    sum_copy(r).start()


def mix_forward(ex, kept, before_all, hidden_all, slope_all, spectral_in, bias, spectral_out):
    a_re, a_im = spectral_in[0, ex.yh], spectral_in[1, ex.yh]
    b_re, b_im = spectral_out[0, ex.yh], spectral_out[1, ex.yh]
    bias_re, bias_im = (
        jnp.broadcast_to(bias[part, pl.ds(ex.yh, 1), :], (BS, BS)).T[:, :1] for part in range(2)
    )

    def mixed(lo, hi):
        real, imaginary = kept[:BS, lo:hi], kept[BS:, lo:hi]
        before = jnp.concatenate(
            [
                dot_tn(a_re, real) - dot_tn(a_im, imaginary) + bias_re,
                dot_tn(a_re, imaginary) + dot_tn(a_im, real) + bias_im,
            ],
            axis=0,
        )
        before_all[:, lo:hi] = before
        cumulative, _ = normal_parts(before)
        hidden = (before * cumulative).astype(BF16)
        hidden_all[:, lo:hi] = hidden
        real, imaginary = hidden[:BS], hidden[BS:]
        second = jnp.concatenate(
            [
                dot_tn(b_re, real) - dot_tn(b_im, imaginary),
                dot_tn(b_re, imaginary) + dot_tn(b_im, real),
            ],
            axis=0,
        )
        slope = jnp.tanh(second * (1.0 / THRESHOLD))
        slope_all[:, lo:hi] = slope
        return second - THRESHOLD * slope

    ex.from_modes(mixed)


def mix_backward(ex, grads, gate, before, slope, spectral_in, spectral_out):
    a_re, a_im = spectral_in[0, ex.yh], spectral_in[1, ex.yh]
    b_re, b_im = spectral_out[0, ex.yh], spectral_out[1, ex.yh]

    def mixed(lo, hi):
        factor = slope[:, lo:hi]
        second = (grads[:, lo:hi].astype(F32) * (factor * factor)).astype(BF16)
        grads[:, lo:hi] = second
        real, imaginary = second[:BS], second[BS:]
        back = jnp.concatenate(
            [
                dot_nn(b_re, real) + dot_nn(b_im, imaginary),
                dot_nn(b_re, imaginary) - dot_nn(b_im, real),
            ],
            axis=0,
        )
        values = before[:, lo:hi]
        cumulative, density = normal_parts(values)
        gated = (back * (cumulative + values * density)).astype(BF16)
        gate[:, lo:hi] = gated
        real, imaginary = gated[:BS], gated[BS:]
        return jnp.concatenate(
            [
                dot_nn(a_re, real) + dot_nn(a_im, imaginary),
                dot_nn(a_re, imaginary) - dot_nn(a_im, real),
            ],
            axis=0,
        )

    ex.from_modes(mixed)


def spectral_sums(ex, sums, kept, gate, hidden, grads):
    sums[...] = jnp.zeros_like(sums)
    low_half, high_half = slice(0, BS), slice(BS, 2 * BS)
    for base, left, right in ((0, kept, gate), (2, hidden, grads)):
        real = dot_nt(left[low_half, :], right[low_half, :]) + dot_nt(
            left[high_half, :], right[high_half, :]
        )
        imaginary = dot_nt(left[low_half, :], right[high_half, :]) - dot_nt(
            left[high_half, :], right[low_half, :]
        )
        for part, value in enumerate((real, imaginary)):
            sums[ex.yh, base + part, :, :, :BS] = value.reshape(4, 24, BS)
    for part in range(2):
        value = jnp.sum(gate[part * BS : (part + 1) * BS, :].astype(F32), axis=1, keepdims=True)
        sums[ex.yh, part, :, :, BS : BS + 1] = value.reshape(4, 24, 1)


def layer_kernel(
    weather, cotangent, width_hbm, weighted_hbm, height_hbm, spectral_in, bias, spectral_out, pin, pout_t,
    output, grad_weather, grad_pin, grad_pout_t, grad_in, grad_out, grad_bias, sum_hbm, *scratch
):
    (normed, filtered, stats, cot, out_block, kept, before, hidden, slope, grads, gate,
     acc_in, acc_out, pin_t, pout, x32, gc, normal_low, cot_low, width, weighted, height,
     cot_sem, out_sem, sum_sem) = scratch[:25]
    scratch = scratch[25:]
    buffers, scratch = scratch[:11], scratch[11:]
    ex = Exchange(buffers, scratch[:12])
    back = Exchange(buffers, scratch[12:24])
    first = Reduction(ex, scratch[24:43], 12)
    other = Reduction(ex, scratch[43:62], 4)
    tables_sem = scratch[62]
    s32 = ex.y32

    def rows_of(r):
        return pl.ds(pl.multiple_of(r * TR, TR), TR)

    def next_cot(r):
        return pltpu.make_async_copy(cotangent.at[:, rows_of(r), :], cot, cot_sem)

    def out_copy(r):
        return pltpu.make_async_copy(out_block, output.at[:, rows_of(r), :], out_sem)

    def sum_copy(r):
        return pltpu.make_async_copy(gc.at[0], sum_hbm.at[r], sum_sem)

    def grad_copy(r):
        return pltpu.make_async_copy(out_block, grad_weather.at[:, rows_of(r), :], out_sem)

    def fetch(at):
        pairs = ((width_hbm, width), (height_hbm, height), (weighted_hbm, weighted))
        return pltpu.make_async_copy(*pairs[at], tables_sem.at[at])

    ex.greet()
    for at in range(3):
        fetch(at).start()
    next_cot(0).start()

    @pl.loop(0, RB)
    def _(r):
        rows = rows_of(r)
        mean = channel_mean(lambda c: weather[c, rows, :].astype(F32))

        def square(c):
            centred = weather[c, rows, :].astype(F32) - mean
            return centred * centred

        spread = lax.rsqrt(channel_mean(square) + EPS)
        stats[0, rows, :] = mean
        stats[1, rows, :] = spread
        for c in range(C):
            normed[c, rows, :] = ((weather[c, rows, :].astype(F32) - mean) * spread).astype(BF16)

    ex.barrier()
    ex.send1(normed)
    pin_t[...] = pin[...].T
    pout[...] = pout_t[...].T
    acc_in[...] = jnp.zeros_like(acc_in)
    acc_out[...] = jnp.zeros_like(acc_out)
    for at in range(3):
        fetch(at).wait()
    ex.width_forward(normed, width, False)
    ex.height_forward(height)
    ex.modes(kept)
    mix_forward(ex, kept, before, hidden, slope, spectral_in, bias, spectral_out)
    ex.height_inverse(height)
    ex.width_inverse(filtered, weighted, True)
    ex.drain(normed, False)

    @pl.loop(0, RB)
    def _(r):
        for d in range(1, 16):
            ex.rowso(filtered, r, d).wait_recv()
        next_cot(r).wait()
        token_rows(
            r, weather, normed, filtered, cot, pin, pin_t, pout, pout_t, acc_in, acc_out,
            s32, x32, gc, normal_low, cot_low, out_block, out_copy, sum_copy, next_cot,
        )
        back.send_rows1(normed, r)

    for half, total in enumerate((acc_in, acc_out)):
        turned = total[...].T
        pieces = jnp.concatenate([turned[:, j * 128 : (j + 1) * 128] for j in range(HID // 128)], axis=0)
        first.src[half] = pieces.reshape(4, 12, 24, 128)
    first.round(0)
    sum_copy(0).wait()
    out_copy(0).wait()
    ex.drain_out(filtered, True)
    first.round(1)
    back.width_forward(normed, weighted, True)
    first.round(2)
    back.height_forward(height)
    first.round(3)
    back.modes(grads)
    mix_backward(back, grads, gate, before, slope, spectral_in, spectral_out)
    first.round(4)
    spectral_sums(back, other.src, kept, gate, hidden, grads)
    other.round(0)
    first.round(5)
    other.round(1)
    back.height_inverse(height)
    other.round(2)
    first.round(6)
    for half, target in enumerate((grad_pin, grad_pout_t)):
        pieces = first.out[half].reshape(HID // 128, C, 128)
        for j in range(HID // 128):
            target[:, j * 128 : (j + 1) * 128] = pieces[j]
    back.width_inverse(filtered, width, False)
    other.round(3)

    def sum_back(r, slot):
        return pltpu.make_async_copy(sum_hbm.at[r], gc.at[slot], sum_sem)

    sum_back(0, 0).start()
    other.round(4)

    @pl.loop(0, NCH)
    def _(i):
        for d in range(1, 16):
            back.copyo(filtered, i, d).wait_recv()

    @pl.loop(0, RB)
    def _(r):
        rows = rows_of(r)
        slot = r % 2
        sum_back(r, slot).wait()

        @pl.when(r < RB - 1)
        def _():
            sum_back(r + 1, 1 - slot).start()

        mean = stats[0, rows, :]
        spread = stats[1, rows, :]

        def own(c):
            return gc[slot, pl.ds(c * TR, TR), :]

        def total(c):
            return own(c) + filtered[c, rows, :].astype(F32)

        def normal(c):
            return (weather[c, rows, :].astype(F32) - mean) * spread

        mean_grad = channel_mean(total)
        mean_cross = channel_mean(lambda c: total(c) * normal(c))

        @pl.when(r > 0)
        def _():
            grad_copy(r).wait()

        for c in range(C):
            inner = total(c) - mean_grad - normal(c) * mean_cross
            out_block[c] = (own(c) + spread * inner).astype(BF16)
        grad_copy(r).start()

    other.round(5)
    other.round(6)
    for block in range(2):
        for part in range(2):
            for base, target in ((0, grad_in), (2, grad_out)):
                target[part, block] = other.out[block, base + part, :, :, :BS].reshape(BS, BS)
            column = other.out[block, part, :, :, BS : BS + 1].reshape(BS, 1)
            grad_bias[part, block : block + 1, :] = jnp.broadcast_to(column, (BS, BS)).T[:1, :]
    back.drain(normed, True)
    back.drain_out(filtered, False)
    grad_copy(0).wait()


def layer_call(*args):
    shape = jax.ShapeDtypeStruct
    dma = pltpu.SemaphoreType.DMA
    vmem, anywhere = (pl.BlockSpec(memory_space=space) for space in (pltpu.VMEM, pl.ANY))
    return pl.pallas_call(
        layer_kernel,
        out_shape=(
            shape((C, LR, LW), BF16),
            shape((C, LR, LW), BF16),
            shape((C, HID), F32),
            shape((C, HID), F32),
            shape((2, NB, BS, BS), F32),
            shape((2, NB, BS, BS), F32),
            shape((2, NB, BS), F32),
            shape((RB, C * TR, LW), F32),
        ),
        in_specs=[vmem] + [anywhere] * 4 + [vmem] * 5,
        out_specs=[anywhere, anywhere] + [vmem] * 5 + [anywhere],
        scratch_shapes=[
            pltpu.VMEM((C, LR, LW), BF16),
            pltpu.VMEM((C, LR, LW), BF16),
            pltpu.VMEM((2, LR, LW), F32),
            pltpu.VMEM((C, TR, LW), BF16),
            pltpu.VMEM((C, TR, LW), BF16),
            pltpu.VMEM((C, MODES), BF16),
            pltpu.VMEM((C, MODES), F32),
            pltpu.VMEM((C, MODES), BF16),
            pltpu.VMEM((C, MODES), F32),
            pltpu.VMEM((C, MODES), BF16),
            pltpu.VMEM((C, MODES), BF16),
            pltpu.VMEM((HID, C), F32),
            pltpu.VMEM((HID, C), F32),
            pltpu.VMEM((HID, C), BF16),
            pltpu.VMEM((HID, C), BF16),
            pltpu.VMEM((C * TR, LW), F32),
            pltpu.VMEM((2, C * TR, LW), F32),
            pltpu.VMEM((C, TN), BF16),
            pltpu.VMEM((C, TN), BF16),
            pltpu.VMEM((2 * KW, W), BF16),
            pltpu.VMEM((2 * KW, W), BF16),
            pltpu.VMEM((H, 2 * KH), BF16),
            dma,
            dma,
            dma,
        ]
        + exchange_scratch()
        + exchange_semaphores()
        + exchange_semaphores()
        + reduction_scratch(12)
        + reduction_scratch(4)
        + [dma((3,))],
        compiler_params=pltpu.CompilerParams(
            collective_id=0, has_side_effects=True, vmem_limit_bytes=67043328
        ),
        name="layer",
    )(*args)


def deliver_kernel(*refs):
    for source, target in zip(refs[:7], refs[7:]):
        target[...] = source[...]


def deliver(arrays):
    steps = 8
    cells = pl.BlockSpec((C // steps, LR, LW), lambda i: (i, 0, 0))
    grads = pl.BlockSpec((C // steps, HID), lambda i: (i, 0))

    def whole(a):
        return pl.BlockSpec(a.shape, lambda i: (0,) * a.ndim)

    specs = [cells, cells, grads, grads] + [whole(a) for a in arrays[4:]]
    return pl.pallas_call(
        deliver_kernel,
        grid=(steps,),
        out_shape=tuple(jax.ShapeDtypeStruct(a.shape, a.dtype) for a in arrays),
        in_specs=specs,
        out_specs=specs,
        name="deliver",
    )(*arrays)


def body(weather, cotangent, spectral_in, spectral_bias, spectral_out, project_in, project_out):
    width, weighted, height = tables()
    results = layer_call(
        weather, cotangent, width, weighted, height, spectral_in, spectral_bias, spectral_out,
        project_in, project_out.T,
    )
    output, grad_weather, grad_pin, grad_pout_t, grad_in, grad_out, grad_bias = deliver(results[:7])
    return output, grad_weather, grad_pin, grad_pout_t.T, grad_in, grad_out, grad_bias


def solution(mesh):
    in_specs = (P(None, "row", "col"), P(None, "row", "col"), P(), P(), P(), P(), P())
    out_specs = (P(None, "row", "col"), P(None, "row", "col"), P(), P(), P(), P(), P())
    return jax.shard_map(body, mesh=mesh, in_specs=in_specs, out_specs=out_specs, check_vma=False)
```

```python
from functools import partial
import math

import numpy as np
import jax
import jax.numpy as jnp
from jax import lax
from jax.experimental import pallas as pl
from jax.experimental.pallas import tpu as pltpu
from jax.sharding import PartitionSpec as P

H = 1024
W = 1024
NB = 2
BS = 96
C = 192
HID = 768
KH = 512
KW = 256

LR = 64
LW = 128
CG = 6
CH = 2
NCH = CG // CH
NX = 4
SG = 4
FG = 2 * KW // SG
RW = 4 * LR
MODES = 2048
TR = 16
RB = LR // TR
TN = TR * LW
CHUNK = 512
EPS = 1e-05
THRESHOLD = 0.1
F32 = jnp.float32
BF16 = jnp.bfloat16
MESH = pl.DeviceIdType.MESH


def tables():
    k = np.arange(KW)
    angle = (k[:, None] * np.arange(W)[None, :] % W).astype(np.float32) * np.float32(2.0 * math.pi / W)
    factor = np.float32(1.0 / math.sqrt(W))
    cosine, sine = np.cos(angle) * factor, -np.sin(angle) * factor
    width = np.stack([cosine.reshape(SG, FG // 2, W), sine.reshape(SG, FG // 2, W)], axis=1).reshape(2 * KW, W)
    weight = np.where(k == 0, 1.0, 2.0).astype(np.float32)[:, None]
    weighted = np.stack(
        [(cosine * weight).reshape(SG, FG // 2, W), (sine * weight).reshape(SG, FG // 2, W)], axis=1
    ).reshape(2 * KW, W)
    m = np.arange(KH)
    frequency = np.where(m < KH // 2, m, m + (H - KH))
    rows = np.arange(H).reshape(2, SG, 2 * LR).transpose(1, 0, 2).reshape(-1)
    angle = (rows[:, None] * frequency[None, :] % H).astype(np.float32) * np.float32(
        2.0 * math.pi / H
    )
    factor = np.float32(1.0 / math.sqrt(H))
    height = np.concatenate([np.cos(angle) * factor, -np.sin(angle) * factor], axis=1)
    return tuple(jnp.asarray(t, F32).astype(BF16) for t in (width, weighted, height))


def dot_nn(left, right):
    return lax.dot_general(left, right, (((1,), (0,)), ((), ())), preferred_element_type=F32)


def dot_nt(left, right):
    return lax.dot_general(left, right, (((1,), (1,)), ((), ())), preferred_element_type=F32)


def dot_tn(left, right):
    return lax.dot_general(left, right, (((0,), (0,)), ((), ())), preferred_element_type=F32)


def normal_parts(values):
    cumulative = 0.5 * (1.0 + lax.erf(values * (1.0 / math.sqrt(2.0))))
    density = jnp.exp(-0.5 * values * values) * (1.0 / math.sqrt(2.0 * math.pi))
    return cumulative, density


class Exchange:
    def __init__(self, buffers, sems):
        (self.X, self.O, self.G, self.K, self.Y0, self.y32, self.Z0, self.Q, self.BK, self.F, self.FO) = buffers
        self.sems = sems
        self.ri = lax.axis_index("row")
        self.ci = lax.axis_index("col")
        self.core = self.ri % 2
        self.s = self.ri // 2
        self.x = self.ci // 2
        self.yh = self.ci % 2
        self.lo = self.s // 4
        self.z = self.s % 4
        self.id1 = (self.ci * 2 + self.lo) * 2 + self.core
        self.part = self.lo * 2 + self.core
        self.id2 = self.x * 4 + self.part
        self.id3 = self.lo * 8 + self.ci

    def peer1(self, d):
        other = (self.id1 + d) % 32
        return other // 4, other % 4

    def peer2(self, e):
        other = (self.id2 + e) % 16
        return other // 4, other % 4

    def peer3(self, d):
        other = (self.id3 + d) % 16
        return other // 8, other % 8

    def row(self, part, z):
        return 2 * (4 * (part // 2) + z) + part % 2

    def greet(self):
        sem = pltpu.get_barrier_semaphore()
        for d in range(1, 32):
            col, part = self.peer1(d)
            pl.semaphore_signal(sem, inc=1, device_id=(self.row(part, self.z), col), device_id_type=MESH)
        for e in range(1, SG):
            z = (self.z + e) % SG
            pl.semaphore_signal(sem, inc=1, device_id=(self.row(self.part, z), self.ci), device_id_type=MESH)

    def barrier(self):
        pl.semaphore_wait(pltpu.get_barrier_semaphore(), 31 + SG - 1)

    def first_channel(self, col, part):
        return (col % 2) * BS + ((col // 2) * 4 + part) * CG

    def rows_at(self, part, start, count):
        return pl.ds(pl.multiple_of(part * LR + start, TR), count)

    def copy1(self, src, i, d):
        col, part = self.peer1(d)
        start = self.first_channel(col, part) + i * CH
        return pltpu.make_async_remote_copy(
            src_ref=src.at[pl.ds(start, CH)],
            dst_ref=self.X.at[self.ci, pl.ds(i * CH, CH), self.rows_at(self.part, 0, LR), :],
            send_sem=self.sems[0].at[i, d],
            recv_sem=self.sems[1].at[i, d],
            device_id=(self.row(part, self.z), col),
            device_id_type=MESH,
        )

    def rows1(self, src, r, d):
        col, part = self.peer1(d)
        return pltpu.make_async_remote_copy(
            src_ref=src.at[pl.ds(self.first_channel(col, part), CG), self.rows_at(0, r * TR, TR), :],
            dst_ref=self.X.at[self.ci, :, self.rows_at(self.part, r * TR, TR), :],
            send_sem=self.sems[0].at[r, d],
            recv_sem=self.sems[1].at[r, d],
            device_id=(self.row(part, self.z), col),
            device_id_type=MESH,
        )

    def send_rows1(self, src, r):
        own = self.first_channel(self.ci, self.part)
        for d in range(1, 32):
            self.rows1(src, r, d).start()
        self.X[self.ci, :, self.rows_at(self.part, r * TR, TR), :] = src[
            pl.ds(own, CG), self.rows_at(0, r * TR, TR), :
        ]

    def send1(self, src):
        own = self.first_channel(self.ci, self.part)

        @pl.loop(0, NCH)
        def _(i):
            for d in range(1, 32):
                self.copy1(src, i, d).start()

        self.X[self.ci, :, self.rows_at(self.part, 0, LR), :] = src[pl.ds(own, CG)]

    def copyb(self, i, e):
        z = (self.z + e) % SG
        return pltpu.make_async_remote_copy(
            src_ref=self.O.at[z, pl.ds(i * CH, CH)],
            dst_ref=self.G.at[self.z, pl.ds(i * CH, CH)],
            send_sem=self.sems[2].at[i, e],
            recv_sem=self.sems[3].at[i, e],
            device_id=(self.row(self.part, z), self.ci),
            device_id_type=MESH,
        )

    def width_forward(self, src, table, by_rows):
        if by_rows:

            @pl.loop(0, RB)
            def _(r):
                for d in range(1, 32):
                    self.rows1(src, r, d).wait_recv()

        @pl.loop(0, NCH)
        def _(i):
            if not by_rows:
                for d in range(1, 32):
                    self.copy1(src, i, d).wait_recv()
            for j in range(CH):
                c = i * CH + j
                field = jnp.concatenate([self.X[p, c] for p in range(8)], axis=1)
                self.O[:, c] = dot_nt(table[...], field).astype(BF16).reshape(SG, FG, RW)
            for e in range(1, SG):
                self.copyb(i, e).start()
            own = pl.ds(i * CH, CH)
            self.G[self.z, own] = self.O[self.z, own]

    def copyc(self, i, e):
        x, part = self.peer2(e)
        return pltpu.make_async_remote_copy(
            src_ref=self.K.at[x, part, pl.ds(i * CH, CH)],
            dst_ref=self.Y0.at[self.id2, pl.ds(i * CH, CH)],
            send_sem=self.sems[4].at[i, e],
            recv_sem=self.sems[5].at[i, e],
            device_id=(self.row(part, self.z), 2 * x + self.yh),
            device_id_type=MESH,
        )

    def height_forward(self, table):
        @pl.loop(0, NCH)
        def _(i):
            for e in range(1, SG):
                self.copyb(i, e).wait_recv()
            own = pl.ds(i * CH, CH)
            spectrum = jnp.concatenate(
                [self.G[z, own].reshape(CH * FG, RW) for z in range(SG)], axis=1
            )
            for x in range(NX):
                lanes = slice(x * 128, (x + 1) * 128)
                shifted = slice(KH + x * 128, KH + (x + 1) * 128)
                both = jnp.concatenate([table[:, lanes], table[:, shifted]], axis=1)
                terms = dot_nn(spectrum, both).reshape(CH, 2, 4, 16, 256)
                real = terms[:, 0, :, :, :128] - terms[:, 1, :, :, 128:]
                imaginary = terms[:, 0, :, :, 128:] + terms[:, 1, :, :, :128]
                for part in range(4):
                    self.K[x, part, own, 0] = real[:, part].astype(BF16)
                    self.K[x, part, own, 1] = imaginary[:, part].astype(BF16)
            for e in range(1, 16):
                self.copyc(i, e).start()
            self.Y0[self.id2, own] = self.K[self.x, self.part, own]

    def modes(self, out):
        @pl.loop(0, NCH)
        def _(i):
            for e in range(1, 16):
                self.copyc(i, e).wait_recv()
        self.y32[...] = self.Y0[...].astype(F32).reshape(BS * 32, 128)
        for part in range(2):
            for k in range(16):
                out[part * BS : (part + 1) * BS, k * 128 : (k + 1) * 128] = self.y32[
                    pl.ds(part * 16 + k, BS, stride=32), :
                ].astype(BF16)

    def copyz(self, i, e):
        x, part = self.peer2(e)
        columns = pl.ds(pl.multiple_of(self.part * 16, 16), 16)
        return pltpu.make_async_remote_copy(
            src_ref=self.Z0.at[x * 4 + part, pl.ds(i * CH, CH)],
            dst_ref=self.Q.at[self.x, pl.ds(i * CH, CH), :, columns, :],
            send_sem=self.sems[6].at[i, e],
            recv_sem=self.sems[7].at[i, e],
            device_id=(self.row(part, self.z), 2 * x + self.yh),
            device_id_type=MESH,
        )

    def from_modes(self, values):
        for q in range(4):
            block = values(q * 512, (q + 1) * 512)
            for part in range(2):
                for j in range(4):
                    self.y32[pl.ds(part * 16 + q * 4 + j, BS, stride=32), :] = block[
                        part * BS : (part + 1) * BS, j * 128 : (j + 1) * 128
                    ]
        self.Z0[...] = self.y32[...].astype(BF16).reshape(16, CG, 2, 16, 128)

        @pl.loop(0, NCH)
        def _(i):
            for e in range(1, 16):
                self.copyz(i, e).start()

        columns = pl.ds(pl.multiple_of(self.part * 16, 16), 16)
        self.Q[self.x, :, :, columns, :] = self.Z0[self.id2]

    def copyf(self, i, e):
        z = (self.z + e) % SG
        return pltpu.make_async_remote_copy(
            src_ref=self.BK.at[z, pl.ds(i * CH, CH)],
            dst_ref=self.F.at[self.z, pl.ds(i * CH, CH)],
            send_sem=self.sems[8].at[i, e],
            recv_sem=self.sems[9].at[i, e],
            device_id=(self.row(self.part, z), self.ci),
            device_id_type=MESH,
        )

    def height_inverse(self, table):
        @pl.loop(0, NCH)
        def _(i):
            for e in range(1, 16):
                self.copyz(i, e).wait_recv()
            own = pl.ds(i * CH, CH)
            modes = jnp.concatenate([self.Q[x, own].reshape(CH * FG, 128) for x in range(NX)], axis=1)
            for z in range(SG):
                rows = slice(z * RW, (z + 1) * RW)
                first = dot_nt(modes, table[rows, :KH]).reshape(CH, 2, FG // 2, RW)
                second = dot_nt(modes, table[rows, KH:]).reshape(CH, 2, FG // 2, RW)
                self.BK[z, own, : FG // 2, :] = (first[:, 0] + second[:, 1]).astype(BF16)
                self.BK[z, own, FG // 2 :, :] = (first[:, 1] - second[:, 0]).astype(BF16)
            for e in range(1, SG):
                self.copyf(i, e).start()
            self.F[self.z, own] = self.BK[self.z, own]

    def copyo(self, out, i, d):
        col, part = self.peer1(d)
        start = self.first_channel(self.ci, self.part) + i * CH
        return pltpu.make_async_remote_copy(
            src_ref=self.FO.at[col, pl.ds(i * CH, CH), self.rows_at(part, 0, LR), :],
            dst_ref=out.at[pl.ds(start, CH)],
            send_sem=self.sems[10].at[i, d],
            recv_sem=self.sems[11].at[i, d],
            device_id=(self.row(part, self.z), col),
            device_id_type=MESH,
        )

    def rowso(self, out, r, d):
        col, part = self.peer1(d)
        start = self.first_channel(self.ci, self.part)
        return pltpu.make_async_remote_copy(
            src_ref=self.FO.at[col, :, self.rows_at(part, r * TR, TR), :],
            dst_ref=out.at[pl.ds(start, CG), self.rows_at(0, r * TR, TR), :],
            send_sem=self.sems[10].at[r, d],
            recv_sem=self.sems[11].at[r, d],
            device_id=(self.row(part, self.z), col),
            device_id_type=MESH,
        )

    def width_inverse(self, out, table, by_rows):
        start = self.first_channel(self.ci, self.part)

        @pl.loop(0, NCH)
        def _(i):
            for e in range(1, SG):
                self.copyf(i, e).wait_recv()
            for j in range(CH):
                c = i * CH + j
                turned = self.F[:, c].reshape(2 * KW, RW).T
                for q in range(4):
                    field = dot_nn(turned, table[:, q * 256 : (q + 1) * 256]).astype(BF16)
                    for half in range(2):
                        self.FO[2 * q + half, c] = field[:, half * 128 : (half + 1) * 128]
            if not by_rows:
                for d in range(1, 32):
                    self.copyo(out, i, d).start()
            out[pl.ds(start + i * CH, CH)] = self.FO[
                self.ci, pl.ds(i * CH, CH), self.rows_at(self.part, 0, LR), :
            ]

        if by_rows:

            @pl.loop(0, RB)
            def _(r):
                for d in range(1, 32):
                    self.rowso(out, r, d).start()

    def drain(self, src, first):
        @pl.loop(0, RB if first else NCH)
        def _(i):
            for d in range(1, 32):
                (self.rows1 if first else self.copy1)(src, i, d).wait_send()

        @pl.loop(0, NCH)
        def _(i):
            for e in range(1, SG):
                self.copyb(i, e).wait_send()
                self.copyf(i, e).wait_send()
            for e in range(1, 16):
                self.copyc(i, e).wait_send()
                self.copyz(i, e).wait_send()

    def drain_out(self, out, by_rows):
        @pl.loop(0, RB if by_rows else NCH)
        def _(i):
            for d in range(1, 32):
                (self.rowso if by_rows else self.copyo)(out, i, d).wait_send()


def exchange_scratch():
    cells = pltpu.VMEM((8, CG, RW, LW), BF16)
    columns = pltpu.VMEM((SG, CG, FG, RW), BF16)
    return [
        cells,
        columns,
        columns,
        pltpu.VMEM((NX, 4, CG, 2, 16, 128), BF16),
        pltpu.VMEM((16, CG, 2, 16, 128), BF16),
        pltpu.VMEM((BS * 32, 128), F32),
        pltpu.VMEM((16, CG, 2, 16, 128), BF16),
        pltpu.VMEM((NX, CG, 2, 64, 128), BF16),
        columns,
        columns,
        cells,
    ]


def exchange_semaphores():
    most = max(NCH, RB)
    pairs = [(most, 32), (NCH, SG), (NCH, 16), (NCH, 16), (NCH, SG), (most, 32)]
    return [pltpu.SemaphoreType.DMA(shape) for shape in pairs for _ in range(2)]


class Reduction:
    def __init__(self, ex, scratch, n):
        self.ex = ex
        self.n = n
        self.src, self.ra, self.t1, self.rb, self.t2, self.rc, self.out = scratch[:7]
        self.sems = scratch[7:19]

    def copy_a(self, dst, src, k):
        ex = self.ex
        return pltpu.make_async_remote_copy(
            src_ref=src,
            dst_ref=dst,
            send_sem=self.sems[k],
            recv_sem=self.sems[k + 1],
            device_id=(2 * ex.s + 1 - ex.core, ex.ci),
            device_id_type=MESH,
        )

    def first_core(self):
        return self.copy_a(self.ra, self.src.at[1 - self.ex.core], 0)

    def last_core(self):
        own = self.out.at[self.ex.core]
        return self.copy_a(own, own, 10)

    def over_z(self, dst, src, k, e):
        ex = self.ex
        return pltpu.make_async_remote_copy(
            src_ref=src,
            dst_ref=dst,
            send_sem=self.sems[k].at[e],
            recv_sem=self.sems[k + 1].at[e],
            device_id=(2 * ((ex.s // 4) * 4 + (ex.z + e) % 4) + ex.core, ex.ci),
            device_id_type=MESH,
        )

    def first_z(self, e):
        return self.over_z(self.rb.at[self.ex.z], self.t1.at[(self.ex.z + e) % 4], 2, e)

    def last_z(self, e):
        own = self.out.at[self.ex.core, self.ex.z]
        return self.over_z(own, own, 8, e)

    def over_rest(self, dst, src, k, d):
        ex = self.ex
        low, col = ex.peer3(d)
        return pltpu.make_async_remote_copy(
            src_ref=src,
            dst_ref=dst,
            send_sem=self.sems[k].at[d],
            recv_sem=self.sems[k + 1].at[d],
            device_id=(2 * (low * 4 + ex.z) + ex.core, col),
            device_id_type=MESH,
        )

    def guard(self, member, action):
        pl.when(member < self.n)(action)

    def peer(self, d):
        return (self.ex.id3 + d) % 16

    def piece_at(self, member):
        return lax.min(member, self.n - 1)

    def first_rest(self, d):
        return self.over_rest(self.rc.at[self.ex.id3], self.t2.at[self.piece_at(self.peer(d))], 4, d)

    def last_rest(self, d, member):
        own = self.out.at[self.ex.core, self.ex.z, self.piece_at(member)]
        return self.over_rest(own, own, 6, d)

    def round(self, number):
        ex = self.ex
        if number == 0:
            self.first_core().start()
        elif number == 1:
            self.first_core().wait_recv()
            self.t1[...] = self.src[ex.core] + self.ra[...]
            for e in range(1, 4):
                self.first_z(e).start()
            self.rb[ex.z] = self.t1[ex.z]
        elif number == 2:
            for e in range(1, 4):
                self.first_z(e).wait_recv()
            self.t2[...] = self.rb[0] + self.rb[1] + self.rb[2] + self.rb[3]
            for d in range(1, 16):
                self.guard(self.peer(d), lambda d=d: self.first_rest(d).start())
            self.guard(ex.id3, self.keep)
        elif number == 3:
            self.guard(ex.id3, self.add)
        elif number == 4:
            for d in range(1, 16):
                source = (ex.id3 + 16 - d) % 16
                self.guard(source, lambda d=d, source=source: self.last_rest(d, source).wait_recv())
            for e in range(1, 4):
                self.last_z(e).start()
        elif number == 5:
            for e in range(1, 4):
                self.last_z(e).wait_recv()
            self.last_core().start()
        else:
            self.last_core().wait_recv()
            self.first_core().wait_send()
            self.last_core().wait_send()
            for e in range(1, 4):
                self.first_z(e).wait_send()
                self.last_z(e).wait_send()
            for d in range(1, 16):
                self.guard(self.peer(d), lambda d=d: self.first_rest(d).wait_send())
            self.guard(ex.id3, self.sent)

    def keep(self):
        self.rc[self.ex.id3] = self.t2[self.piece_at(self.ex.id3)]

    def add(self):
        ex = self.ex
        for d in range(1, 16):
            self.first_rest(d).wait_recv()
        total = self.rc[0]
        for member in range(1, 16):
            total = total + self.rc[member]
        self.out[ex.core, ex.z, self.piece_at(ex.id3)] = total * (1.0 / H)
        for d in range(1, 16):
            self.last_rest(d, ex.id3).start()

    def sent(self):
        for d in range(1, 16):
            self.last_rest(d, self.ex.id3).wait_send()


def reduction_scratch(n):
    dma = pltpu.SemaphoreType.DMA
    part = pltpu.VMEM((4, n, 24, 128), F32)
    whole = pltpu.VMEM((2, 4, n, 24, 128), F32)
    return (
        [whole, part, part, part, pltpu.VMEM((n, 24, 128), F32), pltpu.VMEM((16, 24, 128), F32), whole]
        + [dma] * 2
        + [dma((4,))] * 2
        + [dma((16,))] * 4
        + [dma((4,))] * 2
        + [dma] * 2
    )


def channel_mean(read):
    total = read(0)
    for c in range(1, C):
        total = total + read(c)
    return total * (1.0 / C)


def token_rows(r, weather, normed, filtered, cot, pin, pin_t, pout, pout_t, acc_in, acc_out,
               s32, x32, gc, normal_low, cot_low, output, out_copy, sum_copy, next_cot):
    rows = pl.ds(pl.multiple_of(r * TR, TR), TR)
    g32, c32 = gc.at[0], gc.at[1]

    def at(c):
        return slice(c * TR, (c + 1) * TR)

    total = jnp.zeros((TR, LW), F32)
    for c in range(C):
        value = (
            weather[c, rows, :].astype(F32)
            + normed[c, rows, :].astype(F32)
            + filtered[c, rows, :].astype(F32)
        )
        s32[at(c), :] = value
        total = total + value
        c32[at(c), :] = cot[c].astype(F32)

    @pl.when(r < RB - 1)
    def _():
        next_cot(r + 1).start()

    mean = total * (1.0 / C)

    def square(c):
        centred = s32[at(c), :] - mean
        return centred * centred

    spread = lax.rsqrt(channel_mean(square) + EPS)
    for c in range(C):
        x32[at(c), :] = (s32[at(c), :] - mean) * spread
    for j in range(TR):
        lanes = slice(j * LW, (j + 1) * LW)
        normal_low[:, lanes] = x32[pl.ds(j, C, stride=TR), :].astype(BF16)
        cot_low[:, lanes] = c32[pl.ds(j, C, stride=TR), :].astype(BF16)

    @pl.when(r > 0)
    def _():
        sum_copy(r).wait()
        out_copy(r).wait()

    @pl.loop(0, TN // CHUNK)
    def _(q):
        lanes = pl.ds(pl.multiple_of(q * CHUNK, CHUNK), CHUNK)
        normal = normal_low[:, lanes]
        cot_now = cot_low[:, lanes]
        before = dot_nn(pin_t[...], normal)
        cumulative, density = normal_parts(before)
        hidden = (before * cumulative).astype(BF16)
        back_hidden = dot_nn(pout[...], cot_now)
        back_before = (back_hidden * (cumulative + before * density)).astype(BF16)
        out = dot_nn(pout_t[...], hidden)
        back_normed = dot_nn(pin[...], back_before)
        acc_out[...] += dot_nt(hidden, cot_now)
        acc_in[...] += dot_nt(back_before, normal)
        for j in range(CHUNK // LW):
            sl = slice(j * LW, (j + 1) * LW)
            where = pl.ds(q * (CHUNK // LW) + j, C, stride=TR)
            s32[where, :] += out[:, sl]
            g32[where, :] = back_normed[:, sl]

    for c in range(C):
        output[c] = s32[at(c), :].astype(BF16)
    out_copy(r).start()
    mean_grad = channel_mean(lambda c: g32[at(c), :])
    mean_cross = channel_mean(lambda c: g32[at(c), :] * x32[at(c), :])
    for c in range(C):
        inner = g32[at(c), :] - mean_grad - x32[at(c), :] * mean_cross
        value = c32[at(c), :] + spread * inner
        g32[at(c), :] = value
        normed[c, rows, :] = value.astype(BF16)
    sum_copy(r).start()


def mix_forward(ex, kept, before_all, hidden_all, slope_all, spectral_in, bias, spectral_out):
    a_re, a_im = spectral_in[0, ex.yh], spectral_in[1, ex.yh]
    b_re, b_im = spectral_out[0, ex.yh], spectral_out[1, ex.yh]
    bias_re, bias_im = (
        jnp.broadcast_to(bias[part, pl.ds(ex.yh, 1), :], (BS, BS)).T[:, :1] for part in range(2)
    )

    def mixed(lo, hi):
        real, imaginary = kept[:BS, lo:hi], kept[BS:, lo:hi]
        before = jnp.concatenate(
            [
                dot_tn(a_re, real) - dot_tn(a_im, imaginary) + bias_re,
                dot_tn(a_re, imaginary) + dot_tn(a_im, real) + bias_im,
            ],
            axis=0,
        )
        before_all[:, lo:hi] = before
        cumulative, _ = normal_parts(before)
        hidden = (before * cumulative).astype(BF16)
        hidden_all[:, lo:hi] = hidden
        real, imaginary = hidden[:BS], hidden[BS:]
        second = jnp.concatenate(
            [
                dot_tn(b_re, real) - dot_tn(b_im, imaginary),
                dot_tn(b_re, imaginary) + dot_tn(b_im, real),
            ],
            axis=0,
        )
        slope = jnp.tanh(second * (1.0 / THRESHOLD))
        slope_all[:, lo:hi] = slope
        return second - THRESHOLD * slope

    ex.from_modes(mixed)


def mix_backward(ex, grads, gate, before, slope, spectral_in, spectral_out):
    a_re, a_im = spectral_in[0, ex.yh], spectral_in[1, ex.yh]
    b_re, b_im = spectral_out[0, ex.yh], spectral_out[1, ex.yh]

    def mixed(lo, hi):
        factor = slope[:, lo:hi]
        second = (grads[:, lo:hi].astype(F32) * (factor * factor)).astype(BF16)
        grads[:, lo:hi] = second
        real, imaginary = second[:BS], second[BS:]
        back = jnp.concatenate(
            [
                dot_nn(b_re, real) + dot_nn(b_im, imaginary),
                dot_nn(b_re, imaginary) - dot_nn(b_im, real),
            ],
            axis=0,
        )
        values = before[:, lo:hi]
        cumulative, density = normal_parts(values)
        gated = (back * (cumulative + values * density)).astype(BF16)
        gate[:, lo:hi] = gated
        real, imaginary = gated[:BS], gated[BS:]
        return jnp.concatenate(
            [
                dot_nn(a_re, real) + dot_nn(a_im, imaginary),
                dot_nn(a_re, imaginary) - dot_nn(a_im, real),
            ],
            axis=0,
        )

    ex.from_modes(mixed)


def spectral_sums(ex, sums, kept, gate, hidden, grads):
    sums[...] = jnp.zeros_like(sums)
    low_half, high_half = slice(0, BS), slice(BS, 2 * BS)
    for base, left, right in ((0, kept, gate), (2, hidden, grads)):
        real = dot_nt(left[low_half, :], right[low_half, :]) + dot_nt(
            left[high_half, :], right[high_half, :]
        )
        imaginary = dot_nt(left[low_half, :], right[high_half, :]) - dot_nt(
            left[high_half, :], right[low_half, :]
        )
        for part, value in enumerate((real, imaginary)):
            sums[ex.yh, base + part, :, :, :BS] = value.reshape(4, 24, BS)
    for part in range(2):
        value = jnp.sum(gate[part * BS : (part + 1) * BS, :].astype(F32), axis=1, keepdims=True)
        sums[ex.yh, part, :, :, BS : BS + 1] = value.reshape(4, 24, 1)


def layer_kernel(
    weather, cotangent, width_hbm, weighted_hbm, height_hbm, spectral_in, bias, spectral_out, pin, pout_t,
    output, grad_weather, grad_pin, grad_pout_t, grad_in, grad_out, grad_bias, sum_hbm, *scratch
):
    (normed, filtered, stats, cot, out_block, kept, before, hidden, slope, grads, gate,
     acc_in, acc_out, pin_t, pout, x32, gc, normal_low, cot_low, width, weighted, height,
     cot_sem, out_sem, sum_sem) = scratch[:25]
    scratch = scratch[25:]
    buffers, scratch = scratch[:11], scratch[11:]
    ex = Exchange(buffers, scratch[:12])
    back = Exchange(buffers, scratch[12:24])
    first = Reduction(ex, scratch[24:43], 12)
    other = Reduction(ex, scratch[43:62], 4)
    tables_sem = scratch[62]
    s32 = ex.y32

    def rows_of(r):
        return pl.ds(pl.multiple_of(r * TR, TR), TR)

    def next_cot(r):
        return pltpu.make_async_copy(cotangent.at[:, rows_of(r), :], cot, cot_sem)

    def out_copy(r):
        return pltpu.make_async_copy(out_block, output.at[:, rows_of(r), :], out_sem)

    def sum_copy(r):
        return pltpu.make_async_copy(gc.at[0], sum_hbm.at[r], sum_sem)

    def grad_copy(r):
        return pltpu.make_async_copy(out_block, grad_weather.at[:, rows_of(r), :], out_sem)

    def fetch(at):
        pairs = ((width_hbm, width), (height_hbm, height), (weighted_hbm, weighted))
        return pltpu.make_async_copy(*pairs[at], tables_sem.at[at])

    ex.greet()
    for at in range(3):
        fetch(at).start()
    next_cot(0).start()

    @pl.loop(0, RB)
    def _(r):
        rows = rows_of(r)
        mean = channel_mean(lambda c: weather[c, rows, :].astype(F32))

        def square(c):
            centred = weather[c, rows, :].astype(F32) - mean
            return centred * centred

        spread = lax.rsqrt(channel_mean(square) + EPS)
        stats[0, rows, :] = mean
        stats[1, rows, :] = spread
        for c in range(C):
            normed[c, rows, :] = ((weather[c, rows, :].astype(F32) - mean) * spread).astype(BF16)

    ex.barrier()
    ex.send1(normed)
    pin_t[...] = pin[...].T
    pout[...] = pout_t[...].T
    acc_in[...] = jnp.zeros_like(acc_in)
    acc_out[...] = jnp.zeros_like(acc_out)
    for at in range(3):
        fetch(at).wait()
    ex.width_forward(normed, width, False)
    ex.height_forward(height)
    ex.modes(kept)
    mix_forward(ex, kept, before, hidden, slope, spectral_in, bias, spectral_out)
    ex.height_inverse(height)
    ex.width_inverse(filtered, weighted, True)
    ex.drain(normed, False)

    @pl.loop(0, RB)
    def _(r):
        for d in range(1, 32):
            ex.rowso(filtered, r, d).wait_recv()
        next_cot(r).wait()
        token_rows(
            r, weather, normed, filtered, cot, pin, pin_t, pout, pout_t, acc_in, acc_out,
            s32, x32, gc, normal_low, cot_low, out_block, out_copy, sum_copy, next_cot,
        )
        back.send_rows1(normed, r)

    for half, total in enumerate((acc_in, acc_out)):
        turned = total[...].T
        pieces = jnp.concatenate([turned[:, j * 128 : (j + 1) * 128] for j in range(HID // 128)], axis=0)
        first.src[half] = pieces.reshape(4, 12, 24, 128)
    first.round(0)
    sum_copy(0).wait()
    out_copy(0).wait()
    ex.drain_out(filtered, True)
    first.round(1)
    back.width_forward(normed, weighted, True)
    first.round(2)
    back.height_forward(height)
    first.round(3)
    back.modes(grads)
    mix_backward(back, grads, gate, before, slope, spectral_in, spectral_out)
    first.round(4)
    spectral_sums(back, other.src, kept, gate, hidden, grads)
    other.round(0)
    first.round(5)
    other.round(1)
    back.height_inverse(height)
    other.round(2)
    first.round(6)
    for half, target in enumerate((grad_pin, grad_pout_t)):
        pieces = first.out[half].reshape(HID // 128, C, 128)
        for j in range(HID // 128):
            target[:, j * 128 : (j + 1) * 128] = pieces[j]
    back.width_inverse(filtered, width, False)
    other.round(3)

    def sum_back(r, slot):
        return pltpu.make_async_copy(sum_hbm.at[r], gc.at[slot], sum_sem)

    sum_back(0, 0).start()
    other.round(4)

    @pl.loop(0, NCH)
    def _(i):
        for d in range(1, 32):
            back.copyo(filtered, i, d).wait_recv()

    @pl.loop(0, RB)
    def _(r):
        rows = rows_of(r)
        slot = r % 2
        sum_back(r, slot).wait()

        @pl.when(r < RB - 1)
        def _():
            sum_back(r + 1, 1 - slot).start()

        mean = stats[0, rows, :]
        spread = stats[1, rows, :]

        def own(c):
            return gc[slot, pl.ds(c * TR, TR), :]

        def total(c):
            return own(c) + filtered[c, rows, :].astype(F32)

        def normal(c):
            return (weather[c, rows, :].astype(F32) - mean) * spread

        mean_grad = channel_mean(total)
        mean_cross = channel_mean(lambda c: total(c) * normal(c))

        @pl.when(r > 0)
        def _():
            grad_copy(r).wait()

        for c in range(C):
            inner = total(c) - mean_grad - normal(c) * mean_cross
            out_block[c] = (own(c) + spread * inner).astype(BF16)
        grad_copy(r).start()

    other.round(5)
    other.round(6)
    for block in range(2):
        for part in range(2):
            for base, target in ((0, grad_in), (2, grad_out)):
                target[part, block] = other.out[block, base + part, :, :, :BS].reshape(BS, BS)
            column = other.out[block, part, :, :, BS : BS + 1].reshape(BS, 1)
            grad_bias[part, block : block + 1, :] = jnp.broadcast_to(column, (BS, BS)).T[:1, :]
    back.drain(normed, True)
    back.drain_out(filtered, False)
    grad_copy(0).wait()


def layer_call(*args):
    shape = jax.ShapeDtypeStruct
    dma = pltpu.SemaphoreType.DMA
    vmem, anywhere = (pl.BlockSpec(memory_space=space) for space in (pltpu.VMEM, pl.ANY))
    return pl.pallas_call(
        layer_kernel,
        out_shape=(
            shape((C, LR, LW), BF16),
            shape((C, LR, LW), BF16),
            shape((C, HID), F32),
            shape((C, HID), F32),
            shape((2, NB, BS, BS), F32),
            shape((2, NB, BS, BS), F32),
            shape((2, NB, BS), F32),
            shape((RB, C * TR, LW), F32),
        ),
        in_specs=[vmem] + [anywhere] * 4 + [vmem] * 5,
        out_specs=[anywhere, anywhere] + [vmem] * 5 + [anywhere],
        scratch_shapes=[
            pltpu.VMEM((C, LR, LW), BF16),
            pltpu.VMEM((C, LR, LW), BF16),
            pltpu.VMEM((2, LR, LW), F32),
            pltpu.VMEM((C, TR, LW), BF16),
            pltpu.VMEM((C, TR, LW), BF16),
            pltpu.VMEM((C, MODES), BF16),
            pltpu.VMEM((C, MODES), F32),
            pltpu.VMEM((C, MODES), BF16),
            pltpu.VMEM((C, MODES), F32),
            pltpu.VMEM((C, MODES), BF16),
            pltpu.VMEM((C, MODES), BF16),
            pltpu.VMEM((HID, C), F32),
            pltpu.VMEM((HID, C), F32),
            pltpu.VMEM((HID, C), BF16),
            pltpu.VMEM((HID, C), BF16),
            pltpu.VMEM((C * TR, LW), F32),
            pltpu.VMEM((2, C * TR, LW), F32),
            pltpu.VMEM((C, TN), BF16),
            pltpu.VMEM((C, TN), BF16),
            pltpu.VMEM((2 * KW, W), BF16),
            pltpu.VMEM((2 * KW, W), BF16),
            pltpu.VMEM((H, 2 * KH), BF16),
            dma,
            dma,
            dma,
        ]
        + exchange_scratch()
        + exchange_semaphores()
        + exchange_semaphores()
        + reduction_scratch(12)
        + reduction_scratch(4)
        + [dma((3,))],
        compiler_params=pltpu.CompilerParams(
            collective_id=0, has_side_effects=True, vmem_limit_bytes=67043328
        ),
        name="layer",
    )(*args)


def deliver_kernel(*refs):
    for source, target in zip(refs[:7], refs[7:]):
        target[...] = source[...]


def deliver(arrays):
    steps = 8
    cells = pl.BlockSpec((C // steps, LR, LW), lambda i: (i, 0, 0))
    grads = pl.BlockSpec((C // steps, HID), lambda i: (i, 0))

    def whole(a):
        return pl.BlockSpec(a.shape, lambda i: (0,) * a.ndim)

    specs = [cells, cells, grads, grads] + [whole(a) for a in arrays[4:]]
    return pl.pallas_call(
        deliver_kernel,
        grid=(steps,),
        out_shape=tuple(jax.ShapeDtypeStruct(a.shape, a.dtype) for a in arrays),
        in_specs=specs,
        out_specs=specs,
        name="deliver",
    )(*arrays)


def body(weather, cotangent, spectral_in, spectral_bias, spectral_out, project_in, project_out):
    width, weighted, height = tables()
    results = layer_call(
        weather, cotangent, width, weighted, height, spectral_in, spectral_bias, spectral_out,
        project_in, project_out.T,
    )
    output, grad_weather, grad_pin, grad_pout_t, grad_in, grad_out, grad_bias = deliver(results[:7])
    return output, grad_weather, grad_pin, grad_pout_t.T, grad_in, grad_out, grad_bias


def solution(mesh):
    in_specs = (P(None, "row", "col"), P(None, "row", "col"), P(), P(), P(), P(), P())
    out_specs = (P(None, "row", "col"), P(None, "row", "col"), P(), P(), P(), P(), P())
    return jax.shard_map(body, mesh=mesh, in_specs=in_specs, out_specs=out_specs, check_vma=False)
```
